512 devices in a mesh: grp: 16 (over y, core), seq: 32 (over z, x).
Axes of the slice: x: 4, y: 8, z: 8, core: 2. Of those that a mesh axis runs over, the one named last changes fastest.
Arguments:
- loader_rows: bfloat16 [229376, 3072], P(('grp', 'seq')), may hold values from -6 to 6
- loader_lengths: int32 [16, 32], P('grp', 'seq'), may hold values from 64 to 448, as said below
- net_lengths: int32 [64], replicated, may hold values from 1 to 4096, 131072 in all
- feature_map: float32 [128, 256], replicated, may hold values from -2.5 to 2.5
- carried_state: float32 [8, 256, 128], replicated, may hold values from -18000 to 18000
- carried_norm: float32 [8, 256], replicated, may hold values from 200 to 4000
Outputs:
- attended: float32 [131072, 1024], P(('grp', 'seq'))
The draws below stay inside these ranges and needn't reach their ends.
Inputs may be any that keep to these rules, and one draw needn't show every extreme that they name: `loader_lengths`: in each index of grp the lengths sum to 8192, and the first d of them sum to within 96 of d * 256; rows of a loader shard past its length are padding. `net_lengths`: the lengths sum to 131072.
All inputs are finite; a program needn't handle non-finite values.
Results may differ from the reference program's by a relative error of at most 0.0005.
Values may be sent and summed in bfloat16 or wider, within the bound.
No kernel may reach another device: no remote copies, remote signals or barrier semaphores. Data moves between devices by JAX's collectives and lax.ppermute only.
A program may use at most 128 MiB of HBM per device.

```python
import math
import jax
import jax.numpy as jnp
import numpy as np
from jax import lax

H = 8
DH = 128
M = 256
TOK_DEV = 256
NET_SPAN = 16
DRIFT = 96
CAP = 448
GROUPS = 16
SHARDS = 32
TOKENS = 131072
NETS = 64


def carried_norm_values(key):
    norm_key = jax.random.fold_in(key, 11)
    return jnp.exp(jax.random.uniform(norm_key, (H, M), jnp.float32, math.log(200.0), math.log(4000.0)))


def draw_carried_norm(key, part):
    return carried_norm_values(key)


def draw_carried_state(key, part):
    carried_norms = carried_norm_values(key)
    common = jax.random.truncated_normal(jax.random.fold_in(key, 12), -3.0, 3.0, (H, 1, DH), jnp.float32)
    rough_part = jax.random.truncated_normal(jax.random.fold_in(key, 13), -3.0, 3.0, (H, M, DH), jnp.float32)
    return carried_norms[:, :, None] * (common + 0.5 * rough_part)


def draw_loader_lengths(key, part):
    inner_drift = jax.random.randint(jax.random.fold_in(key, 21), (GROUPS, SHARDS + 1), -DRIFT, DRIFT + 1)
    dip_place = jax.random.randint(jax.random.fold_in(key, 22), (GROUPS, 1), 2, SHARDS - 1)
    column = jnp.arange(SHARDS + 1)[None, :]
    drift_table = jnp.where((column == dip_place - 1) | (column == dip_place + 1), DRIFT, inner_drift)
    drift_table = jnp.where(column == dip_place, -DRIFT, drift_table)
    drift_table = jnp.where((column == 0) | (column == SHARDS), 0, drift_table)
    return (TOK_DEV + drift_table[:, 1:] - drift_table[:, :-1]).astype(jnp.int32)


def block_scale(rng, extent, shards, least, top_value):
    def one(axis_at, parts):
        steps = jax.random.uniform(jax.random.fold_in(jax.random.fold_in(rng, 6), axis_at), (parts,), jnp.float32, least / len(shards), top_value / len(shards))
        return jnp.repeat(jnp.exp(steps), extent[axis_at] // parts).reshape((-1,) + (1,) * (len(extent) - axis_at - 1))

    gain = one(*shards[0])
    for cut in shards[1:]:
        gain = gain * one(*cut)
    return gain


def profile(count, total, reach, lean):
    portions = [(1 << 20) // math.isqrt(standing ** lean) + 1 for standing in range(2, count + 1)]
    surplus, given = total - reach - (count - 1), [1] * (count - 1)
    while surplus > 0:
        movable = [i for i in range(count - 1) if given[i] < reach]
        mass, left = sum([portions[i] for i in movable]), surplus
        for i in movable:
            extra = min(reach - given[i], max(1, left * portions[i] // mass), surplus)
            given[i] = given[i] + extra
            surplus = surplus - extra
    return np.array([reach] + given)


def ragged_sizes(stream_key, number_of, total, bound, skew):
    if number_of == 2:
        one = jax.random.randint(stream_key, (), max(1, total - bound), min(bound, total - 1) + 1)
        return jnp.stack([one, total - one])
    tallies = jnp.asarray(profile(number_of, total, bound, skew), jnp.int32)
    twos = (number_of - 1) // 2
    donor, receiver = tallies[1:1 + 2 * twos:2], tallies[2:2 + 2 * twos:2]
    room = jnp.minimum(donor - 1, bound - receiver)
    shifted = jax.random.randint(jax.random.fold_in(stream_key, 1), (twos,), 0, 1 << 20) % (room + 1)
    tallies = tallies.at[1:1 + 2 * twos:2].set(donor - shifted).at[2:2 + 2 * twos:2].set(receiver + shifted)
    return tallies[jax.random.permutation(jax.random.fold_in(stream_key, 2), number_of)]


def normal_values(stream_key, shape, width, bound, shards=(), kind=jnp.bfloat16):
    values = jax.random.normal(stream_key, shape, jnp.float32) * width
    if len(shards) > 0:
        values = block_scale(stream_key, shape, shards, -0.22, 0.18) * values
    return jnp.clip(values, min=-bound, max=bound).astype(kind)


def setup_inputs(seed: int = 0) -> dict:
    splits = jax.random.split(jax.random.key(seed), 7)
    return {
        "loader_rows": normal_values(splits[0], (GROUPS * SHARDS * CAP, 3 * H * DH), 1.0, 6.0, ((0, 512),)),
        "loader_lengths": draw_loader_lengths(jax.random.fold_in(splits[6], 71), 0),
        "net_lengths": ragged_sizes(splits[2], NETS, TOKENS, NET_SPAN * TOK_DEV, 1).astype(jnp.int32),
        "feature_map": normal_values(splits[3], (DH, M), 1.0, 2.5, (), jnp.float32),
        "carried_state": draw_carried_state(jax.random.fold_in(splits[6], 71), 0),
        "carried_norm": draw_carried_norm(jax.random.fold_in(splits[6], 71), 0),
    }


highest_level = lax.Precision.HIGHEST

def features(split_part, feature_map):
    value_rows = split_part.astype(jnp.float32)
    scale = lax.rsqrt(lax.optimization_barrier(jnp.mean(value_rows * value_rows, axis=-1, keepdims=True)) + 1e-06) * value_rows.shape[-1] ** (-0.5)
    return jnp.exp(jnp.einsum('rhd,dm->rhm', value_rows * scale, feature_map, precision=highest_level))

def net_begins(net_lengths):
    net_ends = jnp.cumsum(net_lengths).astype(jnp.int32)
    begins = net_ends - net_lengths
    return jnp.where(jnp.arange(net_lengths.shape[0]) == 0, -1, begins).astype(jnp.int32)

def local_terms(row_block, positions, valid_rows, begins, feature_map):
    count = row_block.shape[0]
    split_rows = row_block.reshape(count, 3, H, DH)
    query_features = features(split_rows[:, 0], feature_map)
    key_feat = features(split_rows[:, 1], feature_map)
    value_rows = split_rows[:, 2].astype(jnp.float32)
    net_begin = lax.optimization_barrier(jnp.max(jnp.where(begins[None, :] <= positions[:, None], begins[None, :], -1), axis=1)).astype(jnp.int32)
    offsets = jnp.arange(count, dtype=jnp.int32)
    allowed = (net_begin[:, None] == net_begin[None, :]) & (offsets[None, :] <= offsets[:, None]) & valid_rows[None, :]
    scores = jnp.einsum('rhm,shm->hrs', query_features, key_feat, precision=highest_level) * jnp.where(allowed, 1.0, 0.0).astype(jnp.float32)[None]
    numerator_output = jnp.einsum('hrs,shd->rhd', scores, value_rows, precision=highest_level)
    denominator = jnp.transpose(lax.optimization_barrier(jnp.sum(scores, axis=2)))
    last_begin = jnp.max(jnp.where(valid_rows, net_begin, -2))
    weights = jnp.where(valid_rows & (net_begin == last_begin), 1.0, 0.0).astype(jnp.float32)
    weighted_values = key_feat * weights[:, None, None]
    state_running_sum = jnp.einsum('qyu,qyo->yuo', weighted_values, value_rows, precision=highest_level)
    norm_sum = lax.optimization_barrier(jnp.sum(weighted_values, axis=0))
    restart = jnp.max(jnp.where(valid_rows & (net_begin == positions), 1.0, 0.0)).astype(jnp.float32).reshape(1)
    return (numerator_output, denominator, query_features, net_begin, (restart, norm_sum, state_running_sum))

def finish(numerator_output, denominator, query_features, net_begin, valid_rows, block_start, incoming_state, norm_in):
    incoming_carry = jnp.where(net_begin < block_start, 1.0, 0.0).astype(jnp.float32)
    numerator_output = numerator_output + incoming_carry[:, None, None] * jnp.einsum('lqc,qcf->lqf', query_features, incoming_state, precision=highest_level)
    denominator = denominator + incoming_carry[:, None] * jnp.einsum('rhm,hm->rh', query_features, norm_in, precision=highest_level)
    denominator = jnp.where(valid_rows[:, None], denominator, 1.0)
    return (numerator_output / denominator[:, :, None]).reshape(numerator_output.shape[0], -1)

def reference(loader_rows, loader_lengths, net_lengths, feature_map, carried_state, carried_norm):
    shard_sizes = loader_lengths.reshape(-1).astype(jnp.int32)
    shard_begin = (jnp.cumsum(shard_sizes) - shard_sizes).astype(jnp.int32)
    begins = net_begins(net_lengths)
    offsets = jnp.arange(TOK_DEV, dtype=jnp.int32)
    valid_rows = offsets >= 0

    def advance(carried, block_index):
        incoming_state, norm_in = carried
        block_start = (block_index * TOK_DEV).astype(jnp.int32)
        positions = block_start + offsets
        owner_shard = (jnp.searchsorted(shard_begin, positions, side='right') - 1).astype(jnp.int32)
        picked = (owner_shard * CAP + positions - shard_begin[owner_shard]).astype(jnp.int32)
        row_block = loader_rows[picked]
        numerator_output, denominator, query_features, net_begin, element = local_terms(row_block, positions, valid_rows, begins, feature_map)
        attended = finish(numerator_output, denominator, query_features, net_begin, valid_rows, block_start, incoming_state, norm_in)
        restart, norm_sum, state_running_sum = element
        fresh = restart[0] > 0
        new_state = jnp.where(fresh, state_running_sum, incoming_state + state_running_sum)
        new_norm = jnp.where(fresh, norm_sum, norm_in + norm_sum)
        return ((new_state, new_norm), attended)
    blocks = jnp.arange(GROUPS * SHARDS, dtype=jnp.int32)
    final_state, attended = lax.scan(advance, (carried_state, carried_norm), blocks)
    return attended.reshape(TOKENS, H * DH)
```

```python
import functools

import jax
import jax.numpy as jnp
from jax import lax
from jax.experimental import pallas as pl
from jax.experimental.pallas import tpu as pltpu
from jax.sharding import PartitionSpec as P

H = 8
DH = 128
M = 256
TOK_DEV = 256
DRIFT = 96
CAP = 448
SHARDS = 32
DEVICES = 512
GROUP = 8
NETS = 64
TAIL = 112
AUG = 136
HB = 2
F32 = jnp.float32
BF16 = jnp.bfloat16
NT = (((1,), (1,)), ((), ()))


def dot(a, b):
    return jnp.dot(a, b, preferred_element_type=F32)


def dot_nt(a, b):
    return lax.dot_general(a, b, NT, preferred_element_type=F32)


def split(x):
    high = x.astype(BF16)
    return high, (x - high.astype(F32)).astype(BF16)


def tail_start(length):
    start = jnp.maximum(length - DRIFT, 0)
    return jnp.minimum(start - lax.rem(start, 16), CAP - TAIL)


def windows_kernel(length_ref, rows_ref, tail_ref, head_ref, sem):
    start = pl.multiple_of(tail_start(length_ref[0, 0]), 16)
    tail = pltpu.make_async_copy(rows_ref.at[pl.ds(start, TAIL), :], tail_ref, sem.at[0])
    head = pltpu.make_async_copy(rows_ref.at[pl.ds(0, DRIFT), :], head_ref, sem.at[1])
    tail.start()
    head.start()
    tail.wait()
    head.wait()


def windows(rows, length):
    return pl.pallas_call(
        windows_kernel,
        out_shape=(
            jax.ShapeDtypeStruct((TAIL, 3 * H * DH), BF16),
            jax.ShapeDtypeStruct((DRIFT, 3 * H * DH), BF16),
        ),
        in_specs=[pl.BlockSpec(memory_space=pltpu.SMEM), pl.BlockSpec(memory_space=pl.ANY)],
        out_specs=(pl.BlockSpec(memory_space=pl.ANY), pl.BlockSpec(memory_space=pl.ANY)),
        scratch_shapes=[pltpu.SemaphoreType.DMA((2,))],
        name="windows",
    )(length, rows)


def build_selection(lengths_ref, seq_index, own_ref, left_ref, right_ref):
    before = lax.fori_loop(0, seq_index, lambda i, s: s + lengths_ref[i], jnp.int32(0))
    length = lengths_ref[seq_index]
    length_left = lengths_ref[jnp.maximum(seq_index - 1, 0)]
    drift = before - seq_index * TOK_DEV

    def one_hot(width, shift, valid):
        row = lax.broadcasted_iota(jnp.int32, (TOK_DEV, width), 0) - drift
        column = lax.broadcasted_iota(jnp.int32, (TOK_DEV, width), 1)
        return jnp.where((column == row + shift) & valid(row), 1.0, 0.0).astype(BF16)

    own_ref[...] = one_hot(CAP, 0, lambda i: (i >= 0) & (i < length))
    left_ref[...] = one_hot(TAIL, length_left - tail_start(length_left), lambda i: i < 0)
    right_ref[...] = one_hot(DRIFT, -length, lambda i: i >= length)


def pick(selection, pieces):
    total = dot(selection[0][...], pieces[0])
    for one_hot, piece in zip(selection[1:], pieces[1:]):
        total = total + dot(one_hot[...], piece)
    return total


def feature_map_pair(map_ref, pair_ref):
    high, low = split(map_ref[...])
    pair_ref[:DH, :] = high
    pair_ref[DH:, :] = low


def features(part, pair_ref):
    scale = lax.rsqrt(jnp.mean(part * part, axis=-1, keepdims=True) + 1e-06) * DH ** (-0.5)
    twice = part.astype(BF16)
    return jnp.exp(dot(jnp.concatenate([twice, twice], axis=1), pair_ref[...]) * scale)


def state_kernel(
    lengths_ref, where_ref, map_ref, *refs
):
    parts, (out_ref, own, left, right, pair) = refs[:6], refs[6:]

    @pl.when(pl.program_id(0) == 0)
    def _():
        build_selection(lengths_ref, where_ref[0], own, left, right)
        feature_map_pair(map_ref, pair)

    first = where_ref[1]
    valid = lax.broadcasted_iota(jnp.int32, (TOK_DEV, 1), 0) >= first
    norm_rows = jnp.where(
        lax.broadcasted_iota(jnp.int32, (AUG - DH, TOK_DEV), 1) >= first, 1.0, 0.0
    ).astype(BF16)
    keys = pick((own, left, right), [parts[i][...] for i in (0, 2, 4)])
    values = pick((own, left, right), [parts[i][...] for i in (1, 3, 5)])
    for i in range(HB):
        columns = slice(i * DH, (i + 1) * DH)
        high, low = split(features(keys[:, columns], pair))
        masked = jnp.where(valid, values[:, columns], 0.0)
        turned = jnp.concatenate([masked.T.astype(BF16), norm_rows], axis=0)
        out_ref[i] = dot(turned, high) + dot(turned, low)


def part_specs(parts):
    specs = []
    for rows in (CAP, TAIL, DRIFT):
        for part in parts:
            specs.append(
                pl.BlockSpec((rows, HB * DH), lambda i, *_, part=part: (0, part * (H // HB) + i))
            )
    return specs


def selection_scratch():
    return [
        pltpu.VMEM((TOK_DEV, CAP), BF16),
        pltpu.VMEM((TOK_DEV, TAIL), BF16),
        pltpu.VMEM((TOK_DEV, DRIFT), BF16),
        pltpu.VMEM((2 * DH, M), BF16),
    ]


def local_states(lengths, where, feature_map, rows, from_left, from_right):
    return pl.pallas_call(
        state_kernel,
        out_shape=jax.ShapeDtypeStruct((H, AUG, M), F32),
        grid_spec=pltpu.PrefetchScalarGridSpec(
            num_scalar_prefetch=2,
            grid=(H // HB,),
            in_specs=[pl.BlockSpec((DH, M), lambda i, *_: (0, 0))] + part_specs((1, 2)),
            out_specs=pl.BlockSpec((HB, AUG, M), lambda i, *_: (i, 0, 0)),
            scratch_shapes=selection_scratch(),
        ),
        compiler_params=pltpu.CompilerParams(vmem_limit_bytes=32 << 20),
        name="local_states",
    )(lengths, where, feature_map, rows, rows, from_left, from_left, from_right, from_right)


def attention_kernel(lengths_ref, where_ref, begin_ref, map_ref, *refs):
    parts, rest = refs[:9], refs[9:]
    high_ref, low_ref, out_ref, own, left, right, pair = rest

    @pl.when(pl.program_id(0) == 0)
    def _():
        build_selection(lengths_ref, where_ref[0], own, left, right)
        feature_map_pair(map_ref, pair)

    query = lax.broadcasted_iota(jnp.int32, (TOK_DEV, TOK_DEV), 0)
    key = lax.broadcasted_iota(jnp.int32, (TOK_DEV, TOK_DEV), 1)
    allowed = (key <= query) & (key >= begin_ref[...])
    queries, keys, values = (
        pick((own, left, right), [parts[i][...] for i in (j, j + 3, j + 6)]) for j in range(3)
    )
    for i in range(HB):
        columns = slice(i * DH, (i + 1) * DH)
        q_high, q_low = split(features(queries[:, columns], pair))
        k_high, k_low = split(features(keys[:, columns], pair))
        high_ref[i] = q_high
        low_ref[i] = q_low
        scores = dot_nt(q_high, k_high) + dot_nt(q_high, k_low) + dot_nt(q_low, k_high)
        s_high, s_low = split(jnp.where(allowed, scores, 0.0))
        value = jnp.concatenate(
            [values[:, columns].astype(BF16), jnp.ones((TOK_DEV, DH), BF16)], axis=1
        )
        out_ref[i] = dot(s_high, value) + dot(s_low, value)


def local_attention(lengths, where, begin, feature_map, rows, from_left, from_right):
    by_head = pl.BlockSpec((HB, TOK_DEV, M), lambda i, *_: (i, 0, 0))
    return pl.pallas_call(
        attention_kernel,
        out_shape=(
            jax.ShapeDtypeStruct((H, TOK_DEV, M), BF16),
            jax.ShapeDtypeStruct((H, TOK_DEV, M), BF16),
            jax.ShapeDtypeStruct((H, TOK_DEV, 2 * DH), F32),
        ),
        grid_spec=pltpu.PrefetchScalarGridSpec(
            num_scalar_prefetch=2,
            grid=(H // HB,),
            in_specs=[
                pl.BlockSpec((TOK_DEV, 1), lambda i, *_: (0, 0)),
                pl.BlockSpec((DH, M), lambda i, *_: (0, 0)),
            ]
            + part_specs((0, 1, 2)),
            out_specs=(by_head, by_head, by_head),
            scratch_shapes=selection_scratch(),
        ),
        compiler_params=pltpu.CompilerParams(vmem_limit_bytes=48 << 20),
        cost_estimate=pl.CostEstimate(
            flops=6_000_000_000, transcendentals=1_000_000, bytes_accessed=8_000_000
        ),
        name="local_attention",
    )(lengths, where, begin, feature_map, *([rows] * 3), *([from_left] * 3), *([from_right] * 3))


def tail_kernel(where_ref, states_ref, out_ref):
    restart = [where_ref[4 + j] for j in range(GROUP)]
    total = states_ref[0]
    for j in range(1, GROUP):
        keep = restart[j] == 0
        total = jnp.where(keep, total, 0.0) + states_ref[j]
    out_ref[...] = total


def group_tail(where, states):
    return pl.pallas_call(
        tail_kernel,
        out_shape=jax.ShapeDtypeStruct((AUG, M), F32),
        in_specs=[pl.BlockSpec(memory_space=pltpu.SMEM), pl.BlockSpec(memory_space=pltpu.VMEM)],
        out_specs=pl.BlockSpec(memory_space=pltpu.VMEM),
        name="group_tail",
    )(where, states)


def prefix_kernel(
    where_ref, states_ref, near_ref, far_ref, state_ref, norm_ref, out_ref, running
):
    running[...] = near_ref[...] + jnp.where(where_ref[2] == 0, far_ref[...], 0.0)

    @pl.when(where_ref[3] != 0)
    def _():
        running[:DH, :] += state_ref[0].T
        running[DH:, :] += jnp.broadcast_to(norm_ref[0], (AUG - DH, M))

    total = running[...]
    for j in range(GROUP):
        out_ref[j] = total
        total = jnp.where(where_ref[4 + j] == 0, total, 0.0) + states_ref[j]


def entering_states(where, states, near, far, carried_state, carried_norm):
    whole = lambda *shape: pl.BlockSpec(shape, lambda i, *_: (0,) * len(shape))
    return pl.pallas_call(
        prefix_kernel,
        out_shape=jax.ShapeDtypeStruct((GROUP, AUG, M), F32),
        grid_spec=pltpu.PrefetchScalarGridSpec(
            num_scalar_prefetch=1,
            grid=(1,),
            in_specs=[
                whole(GROUP, AUG, M),
                whole(AUG, M),
                whole(AUG, M),
                pl.BlockSpec((1, M, DH), lambda i, where: (where[12], 0, 0)),
                pl.BlockSpec((1, 1, M), lambda i, where: (where[12], 0, 0)),
            ],
            out_specs=whole(GROUP, AUG, M),
            scratch_shapes=[pltpu.VMEM((AUG, M), F32)],
        ),
        name="entering_states",
    )(where, states, near, far, carried_state, carried_norm.reshape(H, 1, M))


def finish_kernel(begin_ref, state_ref, high_ref, low_ref, local_ref, out_ref):
    carried = begin_ref[...] < 0
    for i in range(HB):
        state = jnp.concatenate(
            [state_ref[i, :DH, :], jnp.broadcast_to(state_ref[i, DH : DH + 1, :], (DH, M))], axis=0
        )
        s_high, s_low = split(state)
        q_high = high_ref[i]
        entering = dot_nt(q_high, s_high) + dot_nt(q_high, s_low) + dot_nt(low_ref[i], s_high)
        total = local_ref[i] + jnp.where(carried, entering, 0.0)
        out_ref[:, i * DH : (i + 1) * DH] = total[:, :DH] / total[:, DH:]


def finish(begin, states, high, low, local_sums):
    by_head = pl.BlockSpec((HB, TOK_DEV, M), lambda i: (i, 0, 0))
    return pl.pallas_call(
        finish_kernel,
        out_shape=jax.ShapeDtypeStruct((TOK_DEV, H * DH), F32),
        grid=(H // HB,),
        in_specs=[
            pl.BlockSpec((TOK_DEV, 1), lambda i: (0, 0)),
            pl.BlockSpec((HB, AUG, M), lambda i: (i, 0, 0)),
            by_head,
            by_head,
            by_head,
        ],
        out_specs=pl.BlockSpec((TOK_DEV, HB * DH), lambda i: (0, i)),
        compiler_params=pltpu.CompilerParams(vmem_limit_bytes=32 << 20),
        name="finish",
    )(begin, states, high, low, local_sums)


def shifted(block, axis, count, distance):
    return lax.ppermute(block, axis, [(i - distance, i) for i in range(distance, count)])


def local(loader_rows, loader_lengths, net_lengths, feature_map, carried_state, carried_norm):
    seq_index = lax.axis_index("seq")
    device = lax.axis_index("grp") * SHARDS + seq_index
    start = device * TOK_DEV
    groups = [list(range(i, i + GROUP)) for i in range(0, SHARDS, GROUP)]

    tail_rows, head_rows = windows(loader_rows, loader_lengths)
    from_left = shifted(tail_rows, "seq", SHARDS, 1)
    from_right = lax.ppermute(head_rows, "seq", [(i + 1, i) for i in range(SHARDS - 1)])
    lengths = lax.all_to_all(
        jnp.broadcast_to(loader_lengths.reshape(1), (SHARDS,)), "seq", 0, 0, tiled=True
    )

    begins = jnp.cumsum(net_lengths) - net_lengths
    begins = jnp.where(jnp.arange(NETS) == 0, -1, begins).astype(jnp.int32)
    positions = start + jnp.arange(TOK_DEV, dtype=jnp.int32)
    net_begin = jnp.max(jnp.where(begins[None, :] <= positions[:, None], begins[None, :], -1), axis=1)
    begin = (net_begin - start).astype(jnp.int32)[:, None]
    last_begin = jnp.max(jnp.where(begins < start + TOK_DEV, begins, -1)) - start
    group_start = (device // GROUP) * GROUP
    member = group_start + jnp.arange(GROUP, dtype=jnp.int32)
    restarts = begins // TOK_DEV
    real = jnp.arange(NETS) > 0
    restart = jnp.any((restarts[None, :] == member[:, None]) & real[None, :], axis=1)
    nearby = real & (restarts >= group_start - GROUP) & (restarts < group_start)
    earlier = real & (restarts < group_start)
    where = jnp.concatenate(
        [
            jnp.stack(
                [
                    seq_index,
                    last_begin,
                    jnp.any(nearby).astype(jnp.int32),
                    1 - jnp.any(earlier).astype(jnp.int32),
                ]
            ),
            restart.astype(jnp.int32),
            lax.rem(seq_index, GROUP)[None],
        ]
    ).astype(jnp.int32)

    states = local_states(lengths, where, feature_map, loader_rows, from_left, from_right)
    states = lax.all_to_all(states, "seq", 0, 0, axis_index_groups=groups, tiled=True)
    high, low, sums = local_attention(
        lengths, where, begin, feature_map, loader_rows, from_left, from_right
    )
    states = states.reshape(GROUP, AUG, M)
    tail = group_tail(where, states)
    near = shifted(tail, ("grp", "seq"), DEVICES, GROUP)
    far = shifted(tail, ("grp", "seq"), DEVICES, 2 * GROUP)
    states = entering_states(where, states, near, far, carried_state, carried_norm)
    states = lax.all_to_all(states, "seq", 0, 0, axis_index_groups=groups, tiled=True)
    return finish(begin, states, high, low, sums)


def solution(mesh):
    in_specs = (P(("grp", "seq"), None), P("grp", "seq"), P(), P(), P(), P())
    out_specs = P(("grp", "seq"), None)
    return jax.shard_map(local, mesh=mesh, in_specs=in_specs, out_specs=out_specs, check_vma=False)
```

```python
import functools

import jax
import jax.numpy as jnp
from jax import lax
from jax.experimental import pallas as pl
from jax.experimental.pallas import tpu as pltpu
from jax.sharding import PartitionSpec as P

H = 8
DH = 128
M = 256
TOK_DEV = 256
DRIFT = 96
CAP = 448
SHARDS = 32
DEVICES = 512
GROUP = 8
NETS = 64
TAIL = 104
AUG = 136
HB = 2
HALF = M // 2
F32 = jnp.float32
BF16 = jnp.bfloat16
NT = (((1,), (1,)), ((), ()))


def dot(a, b):
    return jnp.dot(a, b, preferred_element_type=F32)


def dot_nt(a, b):
    return lax.dot_general(a, b, NT, preferred_element_type=F32)


def split(x):
    high = x.astype(BF16)
    return high, (x - high.astype(F32)).astype(BF16)


def tail_start(length):
    start = jnp.maximum(length - DRIFT, 0)
    return jnp.minimum(start - lax.rem(start, 8), CAP - TAIL)


def windows_kernel(length_ref, rows_ref, tail_ref, head_ref, sem):
    start = pl.multiple_of(tail_start(length_ref[0, 0]), 8)
    tail = pltpu.make_async_copy(rows_ref.at[pl.ds(start, TAIL), :], tail_ref, sem.at[0])
    head = pltpu.make_async_copy(rows_ref.at[pl.ds(0, DRIFT), :], head_ref, sem.at[1])
    tail.start()
    head.start()
    tail.wait()
    head.wait()


def windows(rows, length):
    return pl.pallas_call(
        windows_kernel,
        out_shape=(
            jax.ShapeDtypeStruct((TAIL, 3 * H * DH), BF16),
            jax.ShapeDtypeStruct((DRIFT, 3 * H * DH), BF16),
        ),
        in_specs=[pl.BlockSpec(memory_space=pltpu.SMEM), pl.BlockSpec(memory_space=pl.ANY)],
        out_specs=(pl.BlockSpec(memory_space=pltpu.VMEM), pl.BlockSpec(memory_space=pltpu.VMEM)),
        scratch_shapes=[pltpu.SemaphoreType.DMA((2,))],
        name="windows",
    )(length, rows)


def build_selection(lengths_ref, seq_index, own_ref, left_ref, right_ref):
    before = lax.fori_loop(0, seq_index, lambda i, s: s + lengths_ref[i], jnp.int32(0))
    length = lengths_ref[seq_index]
    length_left = lengths_ref[jnp.maximum(seq_index - 1, 0)]
    drift = before - seq_index * TOK_DEV

    def one_hot(width, shift, valid):
        row = lax.broadcasted_iota(jnp.int32, (TOK_DEV, width), 0) - drift
        column = lax.broadcasted_iota(jnp.int32, (TOK_DEV, width), 1)
        return jnp.where((column == row + shift) & valid(row), 1.0, 0.0).astype(BF16)

    own_ref[...] = one_hot(CAP, 0, lambda i: (i >= 0) & (i < length))
    left_ref[...] = one_hot(TAIL, length_left - tail_start(length_left), lambda i: i < 0)
    right_ref[...] = one_hot(DRIFT, -length, lambda i: i >= length)


def pick(selection, pieces):
    total = dot(selection[0][...], pieces[0])
    for one_hot, piece in zip(selection[1:], pieces[1:]):
        total = total + dot(one_hot[...], piece)
    return total


def feature_map_pair(map_ref, pair_ref):
    high, low = split(map_ref[...])
    pair_ref[:DH, :] = high
    pair_ref[DH:, :] = low


def features(part, pair_ref):
    scale = lax.rsqrt(jnp.mean(part * part, axis=-1, keepdims=True) + 1e-06) * DH ** (-0.5)
    twice = part.astype(BF16)
    return jnp.exp(dot(jnp.concatenate([twice, twice], axis=1), pair_ref[...]) * scale)


def state_kernel(
    lengths_ref, where_ref, map_ref, *refs
):
    parts, (out_ref, own, left, right, pair) = refs[:6], refs[6:]

    @pl.when(pl.program_id(0) == 0)
    def _():
        build_selection(lengths_ref, where_ref[0], own, left, right)
        feature_map_pair(map_ref, pair)

    first = where_ref[1]
    valid = lax.broadcasted_iota(jnp.int32, (TOK_DEV, 1), 0) >= first
    norm_rows = jnp.where(
        lax.broadcasted_iota(jnp.int32, (AUG - DH, TOK_DEV), 1) >= first, 1.0, 0.0
    ).astype(BF16)
    keys = pick((own, left, right), [parts[i][...] for i in (0, 2, 4)])
    values = pick((own, left, right), [parts[i][...] for i in (1, 3, 5)])
    for i in range(HB):
        columns = slice(i * DH, (i + 1) * DH)
        high, low = split(features(keys[:, columns], pair))
        masked = jnp.where(valid, values[:, columns], 0.0)
        turned = jnp.concatenate([masked.T.astype(BF16), norm_rows], axis=0)
        out_ref[i] = dot(turned, high) + dot(turned, low)


def part_specs(parts):
    specs = []
    for rows in (CAP, TAIL, DRIFT):
        for part in parts:
            specs.append(
                pl.BlockSpec((rows, HB * DH), lambda i, *_, part=part: (0, part * (H // HB) + i))
            )
    return specs


def selection_scratch():
    return [
        pltpu.VMEM((TOK_DEV, CAP), BF16),
        pltpu.VMEM((TOK_DEV, TAIL), BF16),
        pltpu.VMEM((TOK_DEV, DRIFT), BF16),
        pltpu.VMEM((2 * DH, M), BF16),
    ]


def local_states(lengths, where, feature_map, rows, from_left, from_right):
    return pl.pallas_call(
        state_kernel,
        out_shape=jax.ShapeDtypeStruct((H, AUG, M), F32),
        grid_spec=pltpu.PrefetchScalarGridSpec(
            num_scalar_prefetch=2,
            grid=(H // HB,),
            in_specs=[pl.BlockSpec((DH, M), lambda i, *_: (0, 0))] + part_specs((1, 2)),
            out_specs=pl.BlockSpec((HB, AUG, M), lambda i, *_: (i, 0, 0)),
            scratch_shapes=selection_scratch(),
        ),
        compiler_params=pltpu.CompilerParams(vmem_limit_bytes=32 << 20),
        name="local_states",
    )(lengths, where, feature_map, rows, rows, from_left, from_left, from_right, from_right)


def attention_kernel(lengths_ref, where_ref, begin_ref, map_ref, *refs):
    parts, rest = refs[:9], refs[9:]
    high_ref, low_ref, out_ref, own, left, right, pair = rest

    @pl.when(pl.program_id(0) == 0)
    def _():
        build_selection(lengths_ref, where_ref[0], own, left, right)
        feature_map_pair(map_ref, pair)

    query = lax.broadcasted_iota(jnp.int32, (TOK_DEV, TOK_DEV), 0)
    key = lax.broadcasted_iota(jnp.int32, (TOK_DEV, TOK_DEV), 1)
    allowed = (key <= query) & (key >= begin_ref[...])
    queries, keys, values = (
        pick((own, left, right), [parts[i][...] for i in (j, j + 3, j + 6)]) for j in range(3)
    )
    for i in range(HB):
        columns = slice(i * DH, (i + 1) * DH)
        q_high, q_low = split(features(queries[:, columns], pair))
        k_high, k_low = split(features(keys[:, columns], pair))
        high_ref[i] = q_high
        low_ref[i] = q_low
        scores = dot_nt(q_high, k_high) + dot_nt(q_high, k_low) + dot_nt(q_low, k_high)
        s_high, s_low = split(jnp.where(allowed, scores, 0.0))
        value = jnp.concatenate(
            [values[:, columns].astype(BF16), jnp.ones((TOK_DEV, DH), BF16)], axis=1
        )
        out_ref[i] = dot(s_high, value) + dot(s_low, value)


def local_attention(lengths, where, begin, feature_map, rows, from_left, from_right):
    by_head = pl.BlockSpec((HB, TOK_DEV, M), lambda i, *_: (i, 0, 0))
    return pl.pallas_call(
        attention_kernel,
        out_shape=(
            jax.ShapeDtypeStruct((H, TOK_DEV, M), BF16),
            jax.ShapeDtypeStruct((H, TOK_DEV, M), BF16),
            jax.ShapeDtypeStruct((H, TOK_DEV, 2 * DH), F32),
        ),
        grid_spec=pltpu.PrefetchScalarGridSpec(
            num_scalar_prefetch=2,
            grid=(H // HB,),
            in_specs=[
                pl.BlockSpec((TOK_DEV, 1), lambda i, *_: (0, 0)),
                pl.BlockSpec((DH, M), lambda i, *_: (0, 0)),
            ]
            + part_specs((0, 1, 2)),
            out_specs=(by_head, by_head, by_head),
            scratch_shapes=selection_scratch(),
        ),
        compiler_params=pltpu.CompilerParams(vmem_limit_bytes=48 << 20),
        cost_estimate=pl.CostEstimate(
            flops=6_000_000_000, transcendentals=1_000_000, bytes_accessed=8_000_000
        ),
        name="local_attention",
    )(lengths, where, begin, feature_map, *([rows] * 3), *([from_left] * 3), *([from_right] * 3))


def tail_kernel(where_ref, states_ref, out_ref):
    restart = [where_ref[4 + j] for j in range(GROUP)]
    total = states_ref[0]
    for j in range(1, GROUP):
        keep = restart[j] == 0
        total = jnp.where(keep, total, 0.0) + states_ref[j]
    out_ref[...] = total


def group_tail(where, states):
    return pl.pallas_call(
        tail_kernel,
        out_shape=jax.ShapeDtypeStruct((AUG, M), F32),
        in_specs=[pl.BlockSpec(memory_space=pltpu.SMEM), pl.BlockSpec(memory_space=pltpu.VMEM)],
        out_specs=pl.BlockSpec(memory_space=pltpu.VMEM),
        name="group_tail",
    )(where, states)


def prefix_kernel(
    where_ref, states_ref, near_ref, far_ref, state_ref, norm_ref, out_ref, running
):
    running[...] = near_ref[...] + jnp.where(where_ref[2] == 0, far_ref[...], 0.0)

    @pl.when(where_ref[3] != 0)
    def _():
        running[:DH, :] += state_ref[0].T
        running[DH:, :] += jnp.broadcast_to(norm_ref[0], (AUG - DH, HALF))

    total = running[...]
    for j in range(GROUP):
        out_ref[j] = total
        total = jnp.where(where_ref[4 + j] == 0, total, 0.0) + states_ref[j]


def entering_states(where, states, near, far, carried_state, carried_norm):
    by_group = pl.BlockSpec((GROUP, AUG, HALF), lambda i, where: (0, 0, i))
    one = pl.BlockSpec((AUG, HALF), lambda i, where: (0, i))
    return pl.pallas_call(
        prefix_kernel,
        out_shape=jax.ShapeDtypeStruct((GROUP, AUG, M), F32),
        grid_spec=pltpu.PrefetchScalarGridSpec(
            num_scalar_prefetch=1,
            grid=(M // HALF,),
            in_specs=[
                by_group,
                one,
                one,
                pl.BlockSpec((1, HALF, DH), lambda i, where: (where[12], i, 0)),
                pl.BlockSpec((1, 1, HALF), lambda i, where: (where[12], 0, i)),
            ],
            out_specs=by_group,
            scratch_shapes=[pltpu.VMEM((AUG, HALF), F32)],
        ),
        name="entering_states",
    )(where, states, near, far, carried_state, carried_norm.reshape(H, 1, M))


def finish_kernel(begin_ref, state_ref, high_ref, low_ref, local_ref, out_ref):
    carried = begin_ref[...] < 0
    for i in range(HB):
        state = jnp.concatenate(
            [state_ref[i, :DH, :], jnp.broadcast_to(state_ref[i, DH : DH + 1, :], (DH, M))], axis=0
        )
        s_high, s_low = split(state)
        q_high = high_ref[i]
        entering = dot_nt(q_high, s_high) + dot_nt(q_high, s_low) + dot_nt(low_ref[i], s_high)
        total = local_ref[i] + jnp.where(carried, entering, 0.0)
        out_ref[:, i * DH : (i + 1) * DH] = total[:, :DH] / total[:, DH:]


def finish(begin, states, high, low, local_sums):
    by_head = pl.BlockSpec((HB, TOK_DEV, M), lambda i: (i, 0, 0))
    return pl.pallas_call(
        finish_kernel,
        out_shape=jax.ShapeDtypeStruct((TOK_DEV, H * DH), F32),
        grid=(H // HB,),
        in_specs=[
            pl.BlockSpec((TOK_DEV, 1), lambda i: (0, 0)),
            pl.BlockSpec((HB, AUG, M), lambda i: (i, 0, 0)),
            by_head,
            by_head,
            by_head,
        ],
        out_specs=pl.BlockSpec((TOK_DEV, HB * DH), lambda i: (0, i)),
        compiler_params=pltpu.CompilerParams(vmem_limit_bytes=32 << 20),
        name="finish",
    )(begin, states, high, low, local_sums)


def shifted(block, axis, count, distance):
    return lax.ppermute(block, axis, [(i - distance, i) for i in range(distance, count)])


def local(loader_rows, loader_lengths, net_lengths, feature_map, carried_state, carried_norm):
    seq_index = lax.axis_index("seq")
    device = lax.axis_index("grp") * SHARDS + seq_index
    start = device * TOK_DEV
    groups = [list(range(i, i + GROUP)) for i in range(0, SHARDS, GROUP)]

    tail_rows, head_rows = windows(loader_rows, loader_lengths)
    from_left = shifted(tail_rows, "seq", SHARDS, 1)
    from_right = lax.ppermute(head_rows, "seq", [(i + 1, i) for i in range(SHARDS - 1)])
    lengths = lax.all_to_all(
        jnp.broadcast_to(loader_lengths.reshape(1), (SHARDS,)), "seq", 0, 0, tiled=True
    )

    begins = jnp.cumsum(net_lengths) - net_lengths
    begins = jnp.where(jnp.arange(NETS) == 0, -1, begins).astype(jnp.int32)
    positions = start + jnp.arange(TOK_DEV, dtype=jnp.int32)
    net_begin = jnp.max(jnp.where(begins[None, :] <= positions[:, None], begins[None, :], -1), axis=1)
    begin = (net_begin - start).astype(jnp.int32)[:, None]
    last_begin = jnp.max(jnp.where(begins < start + TOK_DEV, begins, -1)) - start
    group_start = (device // GROUP) * GROUP
    member = group_start + jnp.arange(GROUP, dtype=jnp.int32)
    restarts = begins // TOK_DEV
    real = jnp.arange(NETS) > 0
    restart = jnp.any((restarts[None, :] == member[:, None]) & real[None, :], axis=1)
    nearby = real & (restarts >= group_start - GROUP) & (restarts < group_start)
    earlier = real & (restarts < group_start)
    where = jnp.concatenate(
        [
            jnp.stack(
                [
                    seq_index,
                    last_begin,
                    jnp.any(nearby).astype(jnp.int32),
                    1 - jnp.any(earlier).astype(jnp.int32),
                ]
            ),
            restart.astype(jnp.int32),
            lax.rem(seq_index, GROUP)[None],
        ]
    ).astype(jnp.int32)

    states = local_states(lengths, where, feature_map, loader_rows, from_left, from_right)
    states = lax.all_to_all(states, "seq", 0, 0, axis_index_groups=groups, tiled=True)
    high, low, sums = local_attention(
        lengths, where, begin, feature_map, loader_rows, from_left, from_right
    )
    states, high, low, sums = lax.optimization_barrier((states, high, low, sums))
    tail = group_tail(where, states)
    near = shifted(tail, ("grp", "seq"), DEVICES, GROUP)
    far = shifted(tail, ("grp", "seq"), DEVICES, 2 * GROUP)
    states = entering_states(where, states, near, far, carried_state, carried_norm)
    states = lax.all_to_all(states, "seq", 0, 0, axis_index_groups=groups, tiled=True)
    return finish(begin, states, high, low, sums)


def solution(mesh):
    in_specs = (P(("grp", "seq"), None), P("grp", "seq"), P(), P(), P(), P())
    out_specs = P(("grp", "seq"), None)
    return jax.shard_map(local, mesh=mesh, in_specs=in_specs, out_specs=out_specs, check_vma=False)
```

```python
import functools

import jax
import jax.numpy as jnp
from jax import lax
from jax.experimental import pallas as pl
from jax.experimental.pallas import tpu as pltpu
from jax.sharding import PartitionSpec as P

H = 8
DH = 128
M = 256
TOK_DEV = 256
DRIFT = 96
CAP = 448
SHARDS = 32
DEVICES = 512
GROUP = 8
NETS = 64
TAIL = 104
REST = DRIFT + TAIL
LATER = 128
AUG = 136
CODED = 144
HB = 2
HALF = M // 2
F32 = jnp.float32
BF16 = jnp.bfloat16
I16 = jnp.int16
I32 = jnp.int32
TOP = 32768.0
NT = (((1,), (1,)), ((), ()))


def dot(a, b):
    return jnp.dot(a, b, preferred_element_type=F32)


def dot_nt(a, b):
    return lax.dot_general(a, b, NT, preferred_element_type=F32)


def in_hbm(x):
    return pltpu.with_memory_space_constraint(x, pltpu.HBM)


def split(x):
    high = x.astype(BF16)
    return high, (x - high.astype(F32)).astype(BF16)


def tail_start(length):
    start = jnp.maximum(length - DRIFT, 0)
    return jnp.minimum(start - lax.rem(start, 8), CAP - TAIL)


def windows_kernel(length_ref, rows_ref, tail_ref, head_ref, lengths_ref, sem):
    start = pl.multiple_of(tail_start(length_ref[0, 0]), 8)
    tail = pltpu.make_async_copy(rows_ref.at[pl.ds(start, TAIL), :], tail_ref, sem.at[0])
    head = pltpu.make_async_copy(rows_ref.at[pl.ds(0, DRIFT), :], head_ref, sem.at[1])
    tail.start()
    head.start()
    lengths_ref[...] = jnp.full((SHARDS, 1, 1), length_ref[0, 0], I32)
    tail.wait()
    head.wait()


def windows(rows, length):
    return pl.pallas_call(
        windows_kernel,
        out_shape=(
            jax.ShapeDtypeStruct((TAIL, 3 * H * DH), BF16),
            jax.ShapeDtypeStruct((DRIFT, 3 * H * DH), BF16),
            jax.ShapeDtypeStruct((SHARDS, 1, 1), I32),
        ),
        in_specs=[pl.BlockSpec(memory_space=pltpu.SMEM), pl.BlockSpec(memory_space=pl.ANY)],
        out_specs=[pl.BlockSpec(memory_space=pltpu.VMEM)] * 3,
        scratch_shapes=[pltpu.SemaphoreType.DMA((2,))],
        name="windows",
    )(length, rows)


def flags_kernel(place_ref, nets_ref, out_ref):
    device = place_ref[0]
    start = device * TOK_DEV
    member = lax.rem(device, GROUP)
    group_start = device - member
    for i in range(16):
        out_ref[i] = 0

    def one(n, carry):
        begin, last, first, nearby, earlier = carry
        begin = begin + nets_ref[n - 1]
        row = begin - start
        last = jnp.where(row < TOK_DEV, row, last)
        first = jnp.where(row >= 0, jnp.minimum(first, row), first)
        at = lax.shift_right_logical(begin, 8) - group_start
        inside = (at >= 0) & (at < GROUP)
        out_ref[jnp.where(inside, 4 + at, 15)] = 1
        nearby = jnp.where((at < 0) & (at >= -GROUP), 1, nearby)
        earlier = jnp.where(at < 0, 1, earlier)
        return begin, last, first, nearby, earlier

    zero = jnp.int32(0)
    _, last, first, nearby, earlier = lax.fori_loop(
        1, NETS, one, (zero, -1 - start, jnp.int32(TOK_DEV), zero, zero)
    )
    out_ref[0] = lax.rem(device, SHARDS)
    out_ref[1] = last
    out_ref[2] = nearby
    out_ref[3] = 1 - earlier
    out_ref[12] = member
    out_ref[13] = first
    out_ref[14] = start


def net_flags(place, net_lengths):
    smem = pl.BlockSpec(memory_space=pltpu.SMEM)
    return pl.pallas_call(
        flags_kernel,
        out_shape=jax.ShapeDtypeStruct((16,), I32),
        in_specs=[smem, smem],
        out_specs=smem,
        name="net_flags",
    )(place, net_lengths)


def exponent(top):
    return jnp.ceil(jnp.log2(jnp.maximum(top, 1e-30)))


def encode(state, norm):
    power = exponent(jnp.max(jnp.abs(state), axis=0, keepdims=True))
    codes = jnp.clip(jnp.round(state * jnp.exp2(15.0 - power)), 1.0 - TOP, TOP - 1.0)
    norm_power = exponent(norm)
    scaled = norm * jnp.exp2(15.0 - norm_power)
    high = jnp.minimum(jnp.round(scaled), TOP - 1.0)
    low = jnp.minimum(jnp.round((scaled - high) * TOP), TOP - 1.0)
    row = lax.broadcasted_iota(I32, (CODED - DH, state.shape[1]), 0)
    rest = jnp.where(row == 0, high, jnp.where(row == 1, low, jnp.where(row == 2, power, norm_power)))
    return jnp.concatenate([codes, rest], axis=0).astype(I32).astype(I16)


def decode(coded):
    codes = coded.astype(I32).astype(F32)
    high, low, power, norm_power = (codes[DH + i : DH + i + 1] for i in range(4))
    state = codes[:DH] * jnp.exp2(power - 15.0)
    return state, (high + low * (1.0 / TOP)) * jnp.exp2(norm_power - 15.0)


def build_selection(lengths_ref, seq_index, main_ref, rest_ref, drift_ref):
    before = lax.fori_loop(0, seq_index, lambda i, s: s + lengths_ref[i, 0, 0], jnp.int32(0))
    length = lengths_ref[seq_index, 0, 0]
    length_left = lengths_ref[jnp.maximum(seq_index - 1, 0), 0, 0]
    drift = before - seq_index * TOK_DEV
    drift_ref[0] = drift
    own = lax.broadcasted_iota(I32, (TOK_DEV, TOK_DEV), 0) - drift
    column = lax.broadcasted_iota(I32, (TOK_DEV, TOK_DEV), 1)
    main_ref[...] = jnp.where((column == own) & (own < length), 1.0, 0.0).astype(BF16)
    own = lax.broadcasted_iota(I32, (TOK_DEV, REST), 0) - drift
    column = lax.broadcasted_iota(I32, (TOK_DEV, REST), 1)
    late = jnp.where(drift >= 0, length_left - tail_start(length_left), -TOK_DEV)
    of_right = (own >= length) & (column == own - length) & (column < DRIFT)
    of_left = (column == own + late + DRIFT) & (column >= DRIFT)
    of_left = of_left & (own < jnp.where(drift >= 0, 0, length))
    rest_ref[...] = jnp.where(of_right | of_left, 1.0, 0.0).astype(BF16)


def pick(selection, main, later, left, right):
    main_ref, rest_ref, drift_ref = selection
    other = jnp.where(drift_ref[0] >= 0, left[...], later[:TAIL, :])
    rest = jnp.concatenate([right[...], other], axis=0)
    return dot(main_ref[...], main[...]) + dot(rest_ref[...], rest)


def feature_map_pair(map_ref, pair_ref):
    high, low = split(map_ref[...])
    pair_ref[:DH, :] = high
    pair_ref[DH:, :] = low


def features(part, pair_ref):
    scale = lax.rsqrt(jnp.mean(part * part, axis=-1, keepdims=True) + 1e-06) * DH ** (-0.5)
    twice = part.astype(BF16)
    return jnp.exp(dot(jnp.concatenate([twice, twice], axis=1), pair_ref[...]) * scale)


def state_kernel(where_ref, lengths_ref, map_ref, *refs):
    keys, values, (out_ref, pair, *selection) = refs[:4], refs[4:8], refs[8:]

    @pl.when(pl.program_id(0) == 0)
    def _():
        build_selection(lengths_ref, where_ref[0], *selection)
        feature_map_pair(map_ref, pair)

    first = where_ref[1]
    valid = lax.broadcasted_iota(I32, (TOK_DEV, 1), 0) >= first
    norm_rows = jnp.where(
        lax.broadcasted_iota(I32, (AUG - DH, TOK_DEV), 1) >= first, 1.0, 0.0
    ).astype(BF16)
    keys = pick(selection, *keys)
    values = pick(selection, *values)
    for i in range(HB):
        columns = slice(i * DH, (i + 1) * DH)
        high, low = split(features(keys[:, columns], pair))
        masked = jnp.where(valid, values[:, columns], 0.0)
        turned = jnp.concatenate([masked.T.astype(BF16), norm_rows], axis=0)
        total = dot(turned, high) + dot(turned, low)
        out_ref[i] = encode(total[:DH], total[DH : DH + 1])


def part_specs(part, first):
    column = part * (H // HB) + first
    return [
        pl.BlockSpec((TOK_DEV, HB * DH), lambda i, *_: (0, column + i)),
        pl.BlockSpec((LATER, HB * DH), lambda i, *_: (TOK_DEV // LATER, column + i)),
        pl.BlockSpec((TAIL, HB * DH), lambda i, *_: (0, column + i)),
        pl.BlockSpec((DRIFT, HB * DH), lambda i, *_: (0, column + i)),
    ]


def selection_scratch():
    return [
        pltpu.VMEM((2 * DH, M), BF16),
        pltpu.VMEM((TOK_DEV, TOK_DEV), BF16),
        pltpu.VMEM((TOK_DEV, REST), BF16),
        pltpu.SMEM((1,), I32),
    ]


def local_states(where, lengths, feature_map, rows, left, right):
    smem = pl.BlockSpec(memory_space=pltpu.SMEM)
    return pl.pallas_call(
        state_kernel,
        out_shape=pltpu.HBM((H, CODED, M), I16),
        grid=(H // HB,),
        in_specs=[
            smem,
            smem,
            pl.BlockSpec((DH, M), lambda i: (0, 0)),
            *part_specs(1, 0),
            *part_specs(2, 0),
        ],
        out_specs=pl.BlockSpec((HB, CODED, M), lambda i: (i, 0, 0)),
        scratch_shapes=selection_scratch(),
        compiler_params=pltpu.CompilerParams(vmem_limit_bytes=12 << 20),
        name="local_states",
    )(where, lengths, in_hbm(feature_map), *([rows, rows, left, right] * 2))


def attention_kernel(where_ref, lengths_ref, nets_ref, map_ref, *refs):
    queries, keys, values = refs[:4], refs[4:8], refs[8:12]
    high_ref, low_ref, out_ref, norm_ref, begin_ref, pair, *selection = refs[12:]

    @pl.when(pl.program_id(0) == 0)
    def _():
        build_selection(lengths_ref, where_ref[0], *selection)
        feature_map_pair(map_ref, pair)
        row = lax.broadcasted_iota(I32, (8, TOK_DEV), 1)

        def one(n, carry):
            begin, latest = carry
            begin = begin + nets_ref[n - 1]
            return begin, jnp.where(row >= begin, begin, latest)

        start = where_ref[14]
        _, latest = lax.fori_loop(
            1, NETS, one, (-start, jnp.full((8, TOK_DEV), -1 - start, I32))
        )
        begin_ref[...] = latest.astype(F32).T
        norm_ref[...] = jnp.zeros((TOK_DEV, DH), F32)

    query = lax.broadcasted_iota(I32, (TOK_DEV, TOK_DEV), 0)
    key = lax.broadcasted_iota(I32, (TOK_DEV, TOK_DEV), 1)
    allowed = (key <= query) & (key.astype(F32) >= begin_ref[:, :1])
    lane = lax.broadcasted_iota(I32, (TOK_DEV, DH), 1)
    queries = pick(selection, *queries)
    keys = pick(selection, *keys)
    values = pick(selection, *values)
    for i in range(HB):
        columns = slice(i * DH, (i + 1) * DH)
        q_high, q_low = split(features(queries[:, columns], pair))
        k_high, k_low = split(features(keys[:, columns], pair))
        high_ref[i] = q_high
        low_ref[i] = q_low
        scores = dot_nt(q_high, k_high) + dot_nt(q_high, k_low) + dot_nt(q_low, k_high)
        s_high, s_low = split(jnp.where(allowed, scores, 0.0))
        value = jnp.concatenate(
            [values[:, columns].astype(BF16), jnp.ones((TOK_DEV, DH), BF16)], axis=1
        )
        total = dot(s_high, value) + dot(s_low, value)
        out_ref[i] = total[:, :DH]
        mine = lane == pl.program_id(0) * HB + i
        norm_ref[...] = jnp.where(mine, total[:, DH:], norm_ref[...])


def local_attention(where, lengths, nets, feature_map, rows, left, right, half):
    steps = H // HB // 2
    by_head = lambda width: pl.BlockSpec((HB, TOK_DEV, width), lambda i: (i, 0, 0))
    smem = pl.BlockSpec(memory_space=pltpu.SMEM)
    specs = [spec for part in range(3) for spec in part_specs(part, half * steps)]
    return pl.pallas_call(
        attention_kernel,
        out_shape=(
            pltpu.HBM((H // 2, TOK_DEV, M), BF16),
            pltpu.HBM((H // 2, TOK_DEV, M), BF16),
            pltpu.HBM((H // 2, TOK_DEV, DH), F32),
            pltpu.HBM((TOK_DEV, DH), F32),
        ),
        grid=(steps,),
        in_specs=[smem, smem, smem, pl.BlockSpec((DH, M), lambda i: (0, 0)), *specs],
        out_specs=(
            by_head(M),
            by_head(M),
            by_head(DH),
            pl.BlockSpec((TOK_DEV, DH), lambda i: (0, 0)),
        ),
        scratch_shapes=[pltpu.VMEM((TOK_DEV, 8), F32)] + selection_scratch(),
        compiler_params=pltpu.CompilerParams(vmem_limit_bytes=20 << 20),
        cost_estimate=pl.CostEstimate(
            flops=3_000_000_000, transcendentals=500_000, bytes_accessed=4_000_000
        ),
        name="local_attention",
    )(where, lengths, nets, in_hbm(feature_map), *([rows, rows, left, right] * 3))


def tail_kernel(where_ref, states_ref, out_ref):
    state, norm = decode(states_ref[0])
    for j in range(1, GROUP):
        keep = where_ref[4 + j] == 0
        more, more_norm = decode(states_ref[j])
        state = jnp.where(keep, state, 0.0) + more
        norm = jnp.where(keep, norm, 0.0) + more_norm
    out_ref[...] = encode(state, norm)


def group_tail(where, states):
    vmem = pl.BlockSpec(memory_space=pltpu.VMEM)
    return pl.pallas_call(
        tail_kernel,
        out_shape=jax.ShapeDtypeStruct((CODED, M), I16),
        in_specs=[pl.BlockSpec(memory_space=pltpu.SMEM), vmem],
        out_specs=vmem,
        name="group_tail",
    )(where, states)


def prefix_kernel(
    where_ref, states_ref, near_ref, far_ref, state_ref, norm_ref, out_ref, running, running_norm
):
    near, near_norm = decode(near_ref[...])
    far, far_norm = decode(far_ref[...])
    reaches = where_ref[2] == 0
    running[...] = near + jnp.where(reaches, far, 0.0)
    running_norm[...] = near_norm + jnp.where(reaches, far_norm, 0.0)

    @pl.when(where_ref[3] != 0)
    def _():
        running[...] += state_ref[0].T
        running_norm[...] += norm_ref[0]

    state, norm = running[...], running_norm[...]
    for j in range(GROUP):
        out_ref[j] = encode(state, norm)
        if j < GROUP - 1:
            keep = where_ref[4 + j] == 0
            more, more_norm = decode(states_ref[j])
            state = jnp.where(keep, state, 0.0) + more
            norm = jnp.where(keep, norm, 0.0) + more_norm


def entering_states(where, states, near, far, carried_state, carried_norm):
    by_group = pl.BlockSpec((GROUP, CODED, HALF), lambda i, where: (0, 0, i))
    one = pl.BlockSpec((CODED, HALF), lambda i, where: (0, i))
    return pl.pallas_call(
        prefix_kernel,
        out_shape=jax.ShapeDtypeStruct((GROUP, CODED, M), I16),
        grid_spec=pltpu.PrefetchScalarGridSpec(
            num_scalar_prefetch=1,
            grid=(M // HALF,),
            in_specs=[
                by_group,
                one,
                one,
                pl.BlockSpec((1, HALF, DH), lambda i, where: (where[12], i, 0)),
                pl.BlockSpec((1, 1, HALF), lambda i, where: (where[12], 0, i)),
            ],
            out_specs=by_group,
            scratch_shapes=[pltpu.VMEM((DH, HALF), F32), pltpu.VMEM((1, HALF), F32)],
        ),
        name="entering_states",
    )(where, states, near, far, carried_state, carried_norm.reshape(H, 1, M))


def finish_kernel(where_ref, state_ref, *refs):
    *halves, out_ref = refs
    carried = lax.broadcasted_iota(I32, (TOK_DEV, 1), 0) < where_ref[13]
    lane = lax.broadcasted_iota(I32, (TOK_DEV, DH), 1)
    step = pl.program_id(0)

    def run(high_ref, low_ref, local_ref, local_norm_ref, before):
        for i in range(HB):
            mine = lane == (step - before) * HB + i
            local_norm = jnp.sum(
                jnp.where(mine, local_norm_ref[...], 0.0), axis=1, keepdims=True
            )
            state, norm = decode(state_ref[i])
            state = jnp.concatenate([state, jnp.broadcast_to(norm, (DH, M))], axis=0)
            s_high, s_low = split(state)
            q_high = high_ref[i]
            entering = dot_nt(q_high, s_high) + dot_nt(q_high, s_low) + dot_nt(low_ref[i], s_high)
            entering = jnp.where(carried, entering, 0.0)
            total = local_ref[i] + entering[:, :DH]
            out_ref[:, i * DH : (i + 1) * DH] = total / (local_norm + entering[:, DH:])

    steps = H // HB // 2
    pl.when(step < steps)(lambda: run(*halves[:4], 0))
    pl.when(step >= steps)(lambda: run(*halves[4:], steps))


def finish(where, states, *halves):
    steps = H // HB // 2

    def specs(half):
        top = lambda i: jnp.minimum(i, steps - 1) if half == 0 else jnp.maximum(i - steps, 0)
        by_head = lambda width: pl.BlockSpec((HB, TOK_DEV, width), lambda i: (top(i), 0, 0))
        whole = pl.BlockSpec((TOK_DEV, DH), lambda i: (0, 0))
        return [by_head(M), by_head(M), by_head(DH), whole]

    return pl.pallas_call(
        finish_kernel,
        out_shape=jax.ShapeDtypeStruct((TOK_DEV, H * DH), F32),
        grid=(H // HB,),
        in_specs=[
            pl.BlockSpec(memory_space=pltpu.SMEM),
            pl.BlockSpec((HB, CODED, M), lambda i: (i, 0, 0)),
            *specs(0),
            *specs(1),
        ],
        out_specs=pl.BlockSpec((TOK_DEV, HB * DH), lambda i: (0, i)),
        compiler_params=pltpu.CompilerParams(vmem_limit_bytes=20 << 20),
        name="finish",
    )(where, states, *(in_hbm(half) for half in halves))


def shifted(block, axis, count, distance):
    ahead = max(distance, 0)
    return lax.ppermute(
        block, axis, [(i - distance, i) for i in range(ahead, count + min(distance, 0))]
    )


def local(loader_rows, loader_lengths, net_lengths, feature_map, carried_state, carried_norm):
    device = lax.axis_index("grp") * SHARDS + lax.axis_index("seq")
    groups = [list(range(i, i + GROUP)) for i in range(0, SHARDS, GROUP)]

    tail, head, length = windows(loader_rows, loader_lengths)
    left = shifted(tail, "seq", SHARDS, 1)
    right = shifted(head, "seq", SHARDS, -1)
    lengths = lax.all_to_all(length, "seq", 0, 0, tiled=True)
    where = net_flags(device.astype(I32)[None], net_lengths)
    states = local_states(where, lengths, feature_map, loader_rows, left, right)
    states = lax.all_to_all(states, "seq", 0, 0, axis_index_groups=groups, tiled=True)
    attend = functools.partial(
        local_attention, where, lengths, net_lengths, feature_map, loader_rows, left, right
    )
    first = attend(0)
    states, *first = lax.optimization_barrier((states, *first))
    states = states.reshape(GROUP, CODED, M)
    tail = group_tail(where, states)
    far = shifted(tail, ("grp", "seq"), DEVICES, 2 * GROUP)
    near = shifted(tail, ("grp", "seq"), DEVICES, GROUP)
    second = attend(1)
    near, far, *second = lax.optimization_barrier((near, far, *second))
    states = entering_states(where, states, near, far, carried_state, carried_norm)
    states = lax.all_to_all(states, "seq", 0, 0, axis_index_groups=groups, tiled=True)
    return finish(where, states, *first, *second)


def solution(mesh):
    in_specs = (P(("grp", "seq"), None), P("grp", "seq"), P(), P(), P(), P())
    out_specs = P(("grp", "seq"), None)
    return jax.shard_map(local, mesh=mesh, in_specs=in_specs, out_specs=out_specs, check_vma=False)
```

```python
import functools

import jax
import jax.numpy as jnp
from jax import lax
from jax.experimental import pallas as pl
from jax.experimental.pallas import tpu as pltpu
from jax.sharding import PartitionSpec as P

H = 8
DH = 128
M = 256
TOK_DEV = 256
DRIFT = 96
CAP = 448
SHARDS = 32
DEVICES = 512
GROUP = 8
NETS = 64
TAIL = 104
REST = DRIFT + TAIL
LATER = 128
AUG = 136
CODED = 144
HB = 4
HALF = M // 2
F32 = jnp.float32
BF16 = jnp.bfloat16
I16 = jnp.int16
I32 = jnp.int32
TOP = 32768.0
NT = (((1,), (1,)), ((), ()))


def dot(a, b):
    return jnp.dot(a, b, preferred_element_type=F32)


def dot_nt(a, b):
    return lax.dot_general(a, b, NT, preferred_element_type=F32)


def in_hbm(x):
    return pltpu.with_memory_space_constraint(x, pltpu.HBM)


def split(x):
    high = x.astype(BF16)
    return high, (x - high.astype(F32)).astype(BF16)


def tail_start(length):
    start = jnp.maximum(length - DRIFT, 0)
    return jnp.minimum(start - lax.rem(start, 8), CAP - TAIL)


def windows_kernel(length_ref, rows_ref, tail_ref, head_ref, lengths_ref, sem):
    start = pl.multiple_of(tail_start(length_ref[0, 0]), 8)
    tail = pltpu.make_async_copy(rows_ref.at[pl.ds(start, TAIL), :], tail_ref, sem.at[0])
    head = pltpu.make_async_copy(rows_ref.at[pl.ds(0, DRIFT), :], head_ref, sem.at[1])
    tail.start()
    head.start()
    lengths_ref[...] = jnp.full((SHARDS, 1, 1), length_ref[0, 0], I32)
    tail.wait()
    head.wait()


def windows(rows, length):
    return pl.pallas_call(
        windows_kernel,
        out_shape=(
            jax.ShapeDtypeStruct((TAIL, 3 * H * DH), BF16),
            jax.ShapeDtypeStruct((DRIFT, 3 * H * DH), BF16),
            jax.ShapeDtypeStruct((SHARDS, 1, 1), I32),
        ),
        in_specs=[pl.BlockSpec(memory_space=pltpu.SMEM), pl.BlockSpec(memory_space=pl.ANY)],
        out_specs=[pl.BlockSpec(memory_space=pltpu.VMEM)] * 3,
        scratch_shapes=[pltpu.SemaphoreType.DMA((2,))],
        name="windows",
    )(length, rows)


def flags_kernel(place_ref, nets_ref, out_ref):
    device = place_ref[0]
    start = device * TOK_DEV
    member = lax.rem(device, GROUP)
    group_start = device - member
    for i in range(16):
        out_ref[i] = 0

    def one(n, carry):
        begin, last, first, nearby, earlier = carry
        begin = begin + nets_ref[n - 1]
        row = begin - start
        last = jnp.where(row < TOK_DEV, row, last)
        first = jnp.where(row >= 0, jnp.minimum(first, row), first)
        at = lax.shift_right_logical(begin, 8) - group_start
        inside = (at >= 0) & (at < GROUP)
        out_ref[jnp.where(inside, 4 + at, 15)] = 1
        nearby = jnp.where((at < 0) & (at >= -GROUP), 1, nearby)
        earlier = jnp.where(at < 0, 1, earlier)
        return begin, last, first, nearby, earlier

    zero = jnp.int32(0)
    _, last, first, nearby, earlier = lax.fori_loop(
        1, NETS, one, (zero, -1 - start, jnp.int32(TOK_DEV), zero, zero)
    )
    out_ref[0] = lax.rem(device, SHARDS)
    out_ref[1] = last
    out_ref[2] = nearby
    out_ref[3] = 1 - earlier
    out_ref[12] = member
    out_ref[13] = first
    out_ref[14] = start


def net_flags(place, net_lengths):
    smem = pl.BlockSpec(memory_space=pltpu.SMEM)
    return pl.pallas_call(
        flags_kernel,
        out_shape=jax.ShapeDtypeStruct((16,), I32),
        in_specs=[smem, smem],
        out_specs=smem,
        name="net_flags",
    )(place, net_lengths)


def exponent(top):
    return jnp.ceil(jnp.log2(jnp.maximum(top, 1e-30)))


def encode(state, norm):
    power = exponent(jnp.max(jnp.abs(state), axis=0, keepdims=True))
    codes = jnp.clip(jnp.round(state * jnp.exp2(15.0 - power)), 1.0 - TOP, TOP - 1.0)
    norm_power = exponent(norm)
    scaled = norm * jnp.exp2(15.0 - norm_power)
    high = jnp.minimum(jnp.round(scaled), TOP - 1.0)
    low = jnp.minimum(jnp.round((scaled - high) * TOP), TOP - 1.0)
    row = lax.broadcasted_iota(I32, (CODED - DH, state.shape[1]), 0)
    rest = jnp.where(row == 0, high, jnp.where(row == 1, low, jnp.where(row == 2, power, norm_power)))
    return jnp.concatenate([codes, rest], axis=0).astype(I32).astype(I16)


def decode(coded):
    codes = coded.astype(I32).astype(F32)
    high, low, power, norm_power = (codes[DH + i : DH + i + 1] for i in range(4))
    state = codes[:DH] * jnp.exp2(power - 15.0)
    return state, (high + low * (1.0 / TOP)) * jnp.exp2(norm_power - 15.0)


def build_selection(lengths_ref, seq_index, main_ref, rest_ref, drift_ref):
    before = lax.fori_loop(0, seq_index, lambda i, s: s + lengths_ref[i, 0, 0], jnp.int32(0))
    length = lengths_ref[seq_index, 0, 0]
    length_left = lengths_ref[jnp.maximum(seq_index - 1, 0), 0, 0]
    drift = before - seq_index * TOK_DEV
    drift_ref[0] = drift
    own = lax.broadcasted_iota(I32, (TOK_DEV, TOK_DEV), 0) - drift
    column = lax.broadcasted_iota(I32, (TOK_DEV, TOK_DEV), 1)
    main_ref[...] = jnp.where((column == own) & (own < length), 1.0, 0.0).astype(BF16)
    own = lax.broadcasted_iota(I32, (TOK_DEV, REST), 0) - drift
    column = lax.broadcasted_iota(I32, (TOK_DEV, REST), 1)
    late = jnp.where(drift >= 0, length_left - tail_start(length_left), -TOK_DEV)
    of_right = (own >= length) & (column == own - length) & (column < DRIFT)
    of_left = (column == own + late + DRIFT) & (column >= DRIFT)
    of_left = of_left & (own < jnp.where(drift >= 0, 0, length))
    rest_ref[...] = jnp.where(of_right | of_left, 1.0, 0.0).astype(BF16)


def pick(selection, own, left, right):
    main_ref, rest_ref, drift_ref = selection
    other = jnp.where(drift_ref[0] >= 0, left, own[TOK_DEV : TOK_DEV + TAIL])
    rest = jnp.concatenate([right, other], axis=0)
    return dot(main_ref[...], own[:TOK_DEV]) + dot(rest_ref[...], rest)


def feature_map_pair(map_ref, pair_ref):
    high, low = split(map_ref[...])
    pair_ref[:DH, :] = high
    pair_ref[DH:, :] = low


def features(part, pair_ref):
    scale = lax.rsqrt(jnp.mean(part * part, axis=-1, keepdims=True) + 1e-06) * DH ** (-0.5)
    twice = part.astype(BF16)
    return jnp.exp(dot(jnp.concatenate([twice, twice], axis=1), pair_ref[...]) * scale)


def state_kernel(
    where_ref, lengths_ref, map_ref, rows_ref, left_ref, right_ref, out_ref, pair, *selection
):
    build_selection(lengths_ref, where_ref[0], *selection)
    feature_map_pair(map_ref, pair)
    first = where_ref[1]
    valid = lax.broadcasted_iota(I32, (TOK_DEV, 1), 0) >= first
    norm_rows = jnp.where(
        lax.broadcasted_iota(I32, (AUG - DH, TOK_DEV), 1) >= first, 1.0, 0.0
    ).astype(BF16)
    width = HB * DH
    for at in range(H // HB):
        keys, values = (
            pick(
                selection,
                rows_ref[: TOK_DEV + LATER, start : start + width],
                left_ref[:, start : start + width],
                right_ref[:, start : start + width],
            )
            for start in (H * DH + at * width, 2 * H * DH + at * width)
        )
        for i in range(HB):
            columns = slice(i * DH, (i + 1) * DH)
            high, low = split(features(keys[:, columns], pair))
            masked = jnp.where(valid, values[:, columns], 0.0)
            turned = jnp.concatenate([masked.T.astype(BF16), norm_rows], axis=0)
            total = dot(turned, high) + dot(turned, low)
            out_ref[at * HB + i] = encode(total[:DH], total[DH : DH + 1])


def part_specs(part, first):
    column = part * (H // HB) + first
    return [
        pl.BlockSpec((TOK_DEV + LATER, HB * DH), lambda i, *_: (0, column + i)),
        pl.BlockSpec((TAIL, HB * DH), lambda i, *_: (0, column + i)),
        pl.BlockSpec((DRIFT, HB * DH), lambda i, *_: (0, column + i)),
    ]


def selection_scratch():
    return [
        pltpu.VMEM((2 * DH, M), BF16),
        pltpu.VMEM((TOK_DEV, TOK_DEV), BF16),
        pltpu.VMEM((TOK_DEV, REST), BF16),
        pltpu.SMEM((1,), I32),
    ]


def local_states(where, lengths, feature_map, rows, left, right):
    smem = pl.BlockSpec(memory_space=pltpu.SMEM)
    vmem = pl.BlockSpec(memory_space=pltpu.VMEM)
    whole = lambda *shape: pl.BlockSpec(shape, lambda i: (0,) * len(shape))
    return pl.pallas_call(
        state_kernel,
        out_shape=pltpu.HBM((H, CODED, M), I16),
        grid=(1,),
        in_specs=[smem, smem, whole(DH, M), vmem, vmem, whole(DRIFT, 3 * H * DH)],
        out_specs=whole(H, CODED, M),
        scratch_shapes=selection_scratch(),
        compiler_params=pltpu.CompilerParams(vmem_limit_bytes=24 << 20),
        name="local_states",
    )(where, lengths, in_hbm(feature_map), rows, left, right)


def attention_kernel(where_ref, lengths_ref, nets_ref, map_ref, *refs):
    queries, keys, values = refs[:3], refs[3:6], refs[6:9]
    feature_ref, out_ref, begin_ref, pair, *selection = refs[9:]
    norm_ref = out_ref.at[H // 2]

    @pl.when(pl.program_id(0) == 0)
    def _():
        build_selection(lengths_ref, where_ref[0], *selection)
        feature_map_pair(map_ref, pair)
        row = lax.broadcasted_iota(I32, (8, TOK_DEV), 1)

        def one(n, carry):
            begin, latest = carry
            begin = begin + nets_ref[n - 1]
            return begin, jnp.where(row >= begin, begin, latest)

        start = where_ref[14]
        _, latest = lax.fori_loop(
            1, NETS, one, (-start, jnp.full((8, TOK_DEV), -1 - start, I32))
        )
        begin_ref[...] = latest.astype(F32).T
        norm_ref[...] = jnp.zeros((TOK_DEV, DH), F32)

    query = lax.broadcasted_iota(I32, (TOK_DEV, TOK_DEV), 0)
    key = lax.broadcasted_iota(I32, (TOK_DEV, TOK_DEV), 1)
    allowed = (key <= query) & (key.astype(F32) >= begin_ref[:, :1])
    lane = lax.broadcasted_iota(I32, (TOK_DEV, DH), 1)
    queries, keys, values = (
        pick(selection, *(ref[...] for ref in part)) for part in (queries, keys, values)
    )
    for i in range(HB):
        columns = slice(i * DH, (i + 1) * DH)
        q_high, q_low = split(features(queries[:, columns], pair))
        k_high, k_low = split(features(keys[:, columns], pair))
        feature_ref[i, 0] = q_high
        feature_ref[i, 1] = q_low
        scores = dot_nt(q_high, k_high) + dot_nt(q_high, k_low) + dot_nt(q_low, k_high)
        s_high, s_low = split(jnp.where(allowed, scores, 0.0))
        value = jnp.concatenate(
            [values[:, columns].astype(BF16), jnp.ones((TOK_DEV, DH), BF16)], axis=1
        )
        total = dot(s_high, value) + dot(s_low, value)
        out_ref[i] = total[:, :DH]
        mine = lane == pl.program_id(0) * HB + i
        norm_ref[...] = jnp.where(mine, total[:, DH:], norm_ref[...])


def local_attention(where, lengths, nets, feature_map, rows, left, right, half):
    smem = pl.BlockSpec(memory_space=pltpu.SMEM)
    whole = lambda *shape: pl.BlockSpec(shape, lambda i: (0,) * len(shape))
    specs = [spec for part in range(3) for spec in part_specs(part, half)]
    return pl.pallas_call(
        attention_kernel,
        out_shape=(
            pltpu.HBM((H // 2, 2, TOK_DEV, M), BF16),
            pltpu.HBM((H // 2 + 1, TOK_DEV, DH), F32),
        ),
        grid=(1,),
        in_specs=[smem, smem, smem, whole(DH, M), *specs],
        out_specs=(whole(H // 2, 2, TOK_DEV, M), whole(H // 2 + 1, TOK_DEV, DH)),
        scratch_shapes=[pltpu.VMEM((TOK_DEV, 8), F32)] + selection_scratch(),
        compiler_params=pltpu.CompilerParams(vmem_limit_bytes=24 << 20),
        cost_estimate=pl.CostEstimate(
            flops=3_000_000_000, transcendentals=500_000, bytes_accessed=4_000_000
        ),
        name="local_attention",
    )(where, lengths, nets, in_hbm(feature_map), *([rows, left, right] * 3))


def tail_kernel(where_ref, states_ref, out_ref):
    state, norm = decode(states_ref[0])
    for j in range(1, GROUP):
        keep = where_ref[4 + j] == 0
        more, more_norm = decode(states_ref[j])
        state = jnp.where(keep, state, 0.0) + more
        norm = jnp.where(keep, norm, 0.0) + more_norm
    out_ref[...] = encode(state, norm)


def group_tail(where, states):
    vmem = pl.BlockSpec(memory_space=pltpu.VMEM)
    return pl.pallas_call(
        tail_kernel,
        out_shape=jax.ShapeDtypeStruct((CODED, M), I16),
        in_specs=[pl.BlockSpec(memory_space=pltpu.SMEM), vmem],
        out_specs=vmem,
        name="group_tail",
    )(where, states)


def prefix_kernel(where_ref, states_ref, near_ref, far_ref, state_ref, norm_ref, out_ref, carried, sem):
    near, near_norm = decode(near_ref[...])
    far, far_norm = decode(far_ref[...])
    reaches = where_ref[2] == 0
    state = near + jnp.where(reaches, far, 0.0)
    norm = near_norm + jnp.where(reaches, far_norm, 0.0)
    head = where_ref[12]
    first = where_ref[3] != 0
    carried[...] = jnp.zeros_like(carried)

    @pl.when(first)
    def _():
        copy = pltpu.make_async_copy(state_ref.at[head], carried, sem)
        copy.start()
        copy.wait()

    mine = lax.broadcasted_iota(I32, (H, M), 0) == jnp.where(first, head, -1)
    norm = norm + jnp.sum(jnp.where(mine, norm_ref[...], 0.0), axis=0, keepdims=True)
    state = state + carried[...].T
    for j in range(GROUP):
        out_ref[j] = encode(state, norm)
        if j < GROUP - 1:
            keep = where_ref[4 + j] == 0
            more, more_norm = decode(states_ref[j])
            state = jnp.where(keep, state, 0.0) + more
            norm = jnp.where(keep, norm, 0.0) + more_norm


def entering_states(where, states, near, far, carried_state, carried_norm):
    vmem = pl.BlockSpec(memory_space=pltpu.VMEM)
    return pl.pallas_call(
        prefix_kernel,
        out_shape=jax.ShapeDtypeStruct((GROUP, CODED, M), I16),
        in_specs=[
            pl.BlockSpec(memory_space=pltpu.SMEM),
            vmem,
            vmem,
            vmem,
            pl.BlockSpec(memory_space=pl.ANY),
            vmem,
        ],
        out_specs=vmem,
        scratch_shapes=[pltpu.VMEM((M, DH), F32), pltpu.SemaphoreType.DMA(())],
        name="entering_states",
    )(where, states, near, far, in_hbm(carried_state), carried_norm)


def finish_kernel(where_ref, state_ref, *refs):
    *halves, out_ref = refs
    carried = lax.broadcasted_iota(I32, (TOK_DEV, 1), 0) < where_ref[13]
    lane = lax.broadcasted_iota(I32, (TOK_DEV, DH), 1)

    def run(feature_ref, local_ref):
        norms = local_ref[H // 2]
        for i in range(H // 2):
            local_norm = jnp.sum(jnp.where(lane == i, norms, 0.0), axis=1, keepdims=True)
            state, norm = decode(state_ref[i])
            state = jnp.concatenate([state, jnp.broadcast_to(norm, (DH, M))], axis=0)
            s_high, s_low = split(state)
            q_high, q_low = feature_ref[i, 0], feature_ref[i, 1]
            entering = dot_nt(q_high, s_high) + dot_nt(q_high, s_low) + dot_nt(q_low, s_high)
            entering = jnp.where(carried, entering, 0.0)
            total = local_ref[i] + entering[:, :DH]
            out_ref[:, i * DH : (i + 1) * DH] = total / (local_norm + entering[:, DH:])

    pl.when(pl.program_id(0) == 0)(lambda: run(*halves[:2]))
    pl.when(pl.program_id(0) == 1)(lambda: run(*halves[2:]))


def finish(where, states, *halves):
    half = H // 2
    whole = lambda *shape: pl.BlockSpec(shape, lambda i: (0,) * len(shape))
    return pl.pallas_call(
        finish_kernel,
        out_shape=jax.ShapeDtypeStruct((TOK_DEV, H * DH), F32),
        grid=(2,),
        in_specs=[
            pl.BlockSpec(memory_space=pltpu.SMEM),
            pl.BlockSpec((half, CODED, M), lambda i: (i, 0, 0)),
            *([whole(half, 2, TOK_DEV, M), whole(half + 1, TOK_DEV, DH)] * 2),
        ],
        out_specs=pl.BlockSpec((TOK_DEV, half * DH), lambda i: (0, i)),
        compiler_params=pltpu.CompilerParams(vmem_limit_bytes=24 << 20),
        name="finish",
    )(where, states, *(in_hbm(half) for half in halves))


def shifted(block, axis, count, distance):
    ahead = max(distance, 0)
    return lax.ppermute(
        block, axis, [(i - distance, i) for i in range(ahead, count + min(distance, 0))]
    )


def local(loader_rows, loader_lengths, net_lengths, feature_map, carried_state, carried_norm):
    device = lax.axis_index("grp") * SHARDS + lax.axis_index("seq")
    groups = [list(range(i, i + GROUP)) for i in range(0, SHARDS, GROUP)]

    tail, head, length = windows(loader_rows, loader_lengths)
    left = shifted(tail, "seq", SHARDS, 1)
    right = shifted(head, "seq", SHARDS, -1)
    lengths = lax.all_to_all(length, "seq", 0, 0, tiled=True)
    where = in_hbm(net_flags(device.astype(I32)[None], net_lengths))
    states = local_states(where, lengths, feature_map, loader_rows, left, right)
    states = lax.all_to_all(states, "seq", 0, 0, axis_index_groups=groups, tiled=True)
    attend = functools.partial(
        local_attention, where, lengths, net_lengths, feature_map, loader_rows, left, right
    )
    first = attend(0)
    states, *first = lax.optimization_barrier((states, *first))
    states = states.reshape(GROUP, CODED, M)
    tail = group_tail(where, states)
    far = shifted(tail, ("grp", "seq"), DEVICES, 2 * GROUP)
    near = shifted(tail, ("grp", "seq"), DEVICES, GROUP)
    states = entering_states(where, states, near, far, carried_state, carried_norm)
    states = lax.all_to_all(states, "seq", 0, 0, axis_index_groups=groups, tiled=True)
    return finish(where, states, *first, *attend(1))


def solution(mesh):
    in_specs = (P(("grp", "seq"), None), P("grp", "seq"), P(), P(), P(), P())
    out_specs = P(("grp", "seq"), None)
    return jax.shard_map(local, mesh=mesh, in_specs=in_specs, out_specs=out_specs, check_vma=False)
```

```python
import functools

import jax
import jax.numpy as jnp
from jax import lax
from jax.experimental import pallas as pl
from jax.experimental.pallas import tpu as pltpu
from jax.sharding import PartitionSpec as P

H = 8
DH = 128
M = 256
TOK_DEV = 256
DRIFT = 96
CAP = 448
SHARDS = 32
DEVICES = 512
GROUP = 8
NETS = 64
TAIL = 104
REST = DRIFT + TAIL
LATER = 128
AUG = 136
CODED = 136
HB = 4
HALF = M // 2
F32 = jnp.float32
BF16 = jnp.bfloat16
I16 = jnp.int16
I32 = jnp.int32
TOP = 32768.0
NT = (((1,), (1,)), ((), ()))


def dot(a, b):
    return jnp.dot(a, b, preferred_element_type=F32)


def dot_nt(a, b):
    return lax.dot_general(a, b, NT, preferred_element_type=F32)


def in_hbm(x):
    return pltpu.with_memory_space_constraint(x, pltpu.HBM)


def split(x):
    high = x.astype(BF16)
    return high, (x - high.astype(F32)).astype(BF16)


def tail_start(length):
    start = jnp.maximum(length - DRIFT, 0)
    return jnp.minimum(start - lax.rem(start, 8), CAP - TAIL)


def windows_kernel(length_ref, rows_ref, tail_ref, head_ref, lengths_ref, sem):
    start = pl.multiple_of(tail_start(length_ref[0, 0]), 8)
    tail = pltpu.make_async_copy(rows_ref.at[pl.ds(start, TAIL), :], tail_ref, sem.at[0])
    head = pltpu.make_async_copy(rows_ref.at[pl.ds(0, DRIFT), :], head_ref, sem.at[1])
    tail.start()
    head.start()
    lengths_ref[...] = jnp.full((SHARDS, 1, 1), length_ref[0, 0], I32)
    tail.wait()
    head.wait()


def windows(rows, length):
    return pl.pallas_call(
        windows_kernel,
        out_shape=(
            jax.ShapeDtypeStruct((TAIL, 3 * H * DH), BF16),
            jax.ShapeDtypeStruct((DRIFT, 3 * H * DH), BF16),
            jax.ShapeDtypeStruct((SHARDS, 1, 1), I32),
        ),
        in_specs=[pl.BlockSpec(memory_space=pltpu.SMEM), pl.BlockSpec(memory_space=pl.ANY)],
        out_specs=[pl.BlockSpec(memory_space=pltpu.VMEM)] * 3,
        scratch_shapes=[pltpu.SemaphoreType.DMA((2,))],
        name="windows",
    )(length, rows)


def flags_kernel(place_ref, nets_ref, out_ref):
    device = place_ref[0]
    start = device * TOK_DEV
    member = lax.rem(device, GROUP)
    group_start = device - member
    for i in range(16):
        out_ref[i] = 0

    def one(n, carry):
        begin, last, first, nearby, earlier = carry
        begin = begin + nets_ref[n - 1]
        row = begin - start
        last = jnp.where(row < TOK_DEV, row, last)
        first = jnp.where(row >= 0, jnp.minimum(first, row), first)
        at = lax.shift_right_logical(begin, 8) - group_start
        inside = (at >= 0) & (at < GROUP)
        out_ref[jnp.where(inside, 4 + at, 15)] = 1
        nearby = jnp.where((at < 0) & (at >= -GROUP), 1, nearby)
        earlier = jnp.where(at < 0, 1, earlier)
        return begin, last, first, nearby, earlier

    zero = jnp.int32(0)
    _, last, first, nearby, earlier = lax.fori_loop(
        1, NETS, one, (zero, -1 - start, jnp.int32(TOK_DEV), zero, zero)
    )
    out_ref[0] = lax.rem(device, SHARDS)
    out_ref[1] = last
    out_ref[2] = nearby
    out_ref[3] = 1 - earlier
    out_ref[12] = member
    out_ref[13] = first
    out_ref[14] = start


def net_flags(place, net_lengths):
    smem = pl.BlockSpec(memory_space=pltpu.SMEM)
    return pl.pallas_call(
        flags_kernel,
        out_shape=jax.ShapeDtypeStruct((16,), I32),
        in_specs=[smem, smem],
        out_specs=smem,
        name="net_flags",
    )(place, net_lengths)


def exponent(top):
    return jnp.ceil(jnp.log2(jnp.maximum(top, 1e-30)))


def encode(state, norm):
    power = exponent(jnp.max(jnp.abs(state), axis=0, keepdims=True))
    codes = jnp.clip(jnp.round(state * jnp.exp2(15.0 - power)), 1.0 - TOP, TOP - 1.0)
    norm_power = exponent(norm)
    scaled = norm * jnp.exp2(15.0 - norm_power)
    high = jnp.minimum(jnp.round(scaled), TOP - 1.0)
    low = jnp.minimum(jnp.round((scaled - high) * TOP), TOP - 1.0)
    row = lax.broadcasted_iota(I32, (CODED - DH, state.shape[1]), 0)
    rest = jnp.where(row == 0, high, jnp.where(row == 1, low, jnp.where(row == 2, power, norm_power)))
    return jnp.concatenate([codes, rest], axis=0).astype(I32).astype(I16)


def decode(coded):
    codes = coded.astype(I32).astype(F32)
    high, low, power, norm_power = (codes[DH + i : DH + i + 1] for i in range(4))
    state = codes[:DH] * jnp.exp2(power - 15.0)
    return state, (high + low * (1.0 / TOP)) * jnp.exp2(norm_power - 15.0)


def build_selection(lengths_ref, seq_index, main_ref, rest_ref, drift_ref):
    before = lax.fori_loop(0, seq_index, lambda i, s: s + lengths_ref[i, 0, 0], jnp.int32(0))
    length = lengths_ref[seq_index, 0, 0]
    length_left = lengths_ref[jnp.maximum(seq_index - 1, 0), 0, 0]
    drift = before - seq_index * TOK_DEV
    drift_ref[0] = drift
    own = lax.broadcasted_iota(I32, (TOK_DEV, TOK_DEV), 0) - drift
    column = lax.broadcasted_iota(I32, (TOK_DEV, TOK_DEV), 1)
    main_ref[...] = jnp.where((column == own) & (own < length), 1.0, 0.0).astype(BF16)
    own = lax.broadcasted_iota(I32, (TOK_DEV, REST), 0) - drift
    column = lax.broadcasted_iota(I32, (TOK_DEV, REST), 1)
    late = jnp.where(drift >= 0, length_left - tail_start(length_left), -TOK_DEV)
    of_right = (own >= length) & (column == own - length) & (column < DRIFT)
    of_left = (column == own + late + DRIFT) & (column >= DRIFT)
    of_left = of_left & (own < jnp.where(drift >= 0, 0, length))
    rest_ref[...] = jnp.where(of_right | of_left, 1.0, 0.0).astype(BF16)


def pick(selection, own, left, right):
    main_ref, rest_ref, drift_ref = selection
    other = jnp.where(drift_ref[0] >= 0, left, own[TOK_DEV : TOK_DEV + TAIL])
    rest = jnp.concatenate([right, other], axis=0)
    return dot(main_ref[...], own[:TOK_DEV]) + dot(rest_ref[...], rest)


def feature_map_pair(map_ref, pair_ref):
    high, low = split(map_ref[...])
    pair_ref[:DH, :] = high
    pair_ref[DH:, :] = low


def features(part, pair_ref):
    scale = lax.rsqrt(jnp.mean(part * part, axis=-1, keepdims=True) + 1e-06) * DH ** (-0.5)
    twice = part.astype(BF16)
    return jnp.exp(dot(jnp.concatenate([twice, twice], axis=1), pair_ref[...]) * scale)


def state_kernel(
    where_ref, lengths_ref, map_ref, rows_ref, left_ref, right_ref, out_ref, pair, *selection
):
    build_selection(lengths_ref, where_ref[0], *selection)
    feature_map_pair(map_ref, pair)
    first = where_ref[1]
    valid = lax.broadcasted_iota(I32, (TOK_DEV, 1), 0) >= first
    norm_rows = jnp.where(
        lax.broadcasted_iota(I32, (AUG - DH, TOK_DEV), 1) >= first, 1.0, 0.0
    ).astype(BF16)
    width = HB * DH
    for at in range(H // HB):
        keys, values = (
            pick(
                selection,
                rows_ref[: TOK_DEV + LATER, start : start + width],
                left_ref[:, start : start + width],
                right_ref[:, start : start + width],
            )
            for start in (H * DH + at * width, 2 * H * DH + at * width)
        )
        for i in range(HB):
            columns = slice(i * DH, (i + 1) * DH)
            high, low = split(features(keys[:, columns], pair))
            masked = jnp.where(valid, values[:, columns], 0.0)
            turned = jnp.concatenate([masked.T.astype(BF16), norm_rows], axis=0)
            total = dot(turned, high) + dot(turned, low)
            out_ref[at * HB + i] = encode(total[:DH], total[DH : DH + 1])


def part_specs(part, first):
    column = part * (H // HB) + first
    return [
        pl.BlockSpec((TOK_DEV + LATER, HB * DH), lambda i, *_: (0, column + i)),
        pl.BlockSpec((TAIL, HB * DH), lambda i, *_: (0, column + i)),
        pl.BlockSpec((DRIFT, HB * DH), lambda i, *_: (0, column + i)),
    ]


def selection_scratch():
    return [
        pltpu.VMEM((2 * DH, M), BF16),
        pltpu.VMEM((TOK_DEV, TOK_DEV), BF16),
        pltpu.VMEM((TOK_DEV, REST), BF16),
        pltpu.SMEM((1,), I32),
    ]


def local_states(where, lengths, feature_map, rows, left, right):
    smem = pl.BlockSpec(memory_space=pltpu.SMEM)
    vmem = pl.BlockSpec(memory_space=pltpu.VMEM)
    whole = lambda *shape: pl.BlockSpec(shape, lambda i: (0,) * len(shape))
    return pl.pallas_call(
        state_kernel,
        out_shape=pltpu.HBM((H, CODED, M), I16),
        grid=(1,),
        in_specs=[smem, smem, whole(DH, M), vmem, vmem, whole(DRIFT, 3 * H * DH)],
        out_specs=whole(H, CODED, M),
        scratch_shapes=selection_scratch(),
        compiler_params=pltpu.CompilerParams(vmem_limit_bytes=24 << 20),
        name="local_states",
    )(where, lengths, in_hbm(feature_map), rows, left, right)


def attention_kernel(where_ref, lengths_ref, nets_ref, map_ref, *refs):
    queries, keys, values = refs[:3], refs[3:6], refs[6:9]
    feature_ref, sums_ref, begin_ref, pair, *selection = refs[-7:]
    out_ref = sums_ref.at[0]
    norm_ref = out_ref.at[H // 2]

    @pl.when(pl.program_id(0) == 0)
    def _():
        build_selection(lengths_ref, where_ref[0], *selection)
        feature_map_pair(map_ref, pair)
        row = lax.broadcasted_iota(I32, (8, TOK_DEV), 1)

        def one(n, carry):
            begin, latest = carry
            begin = begin + nets_ref[n - 1]
            return begin, jnp.where(row >= begin, begin, latest)

        start = where_ref[14]
        _, latest = lax.fori_loop(
            1, NETS, one, (-start, jnp.full((8, TOK_DEV), -1 - start, I32))
        )
        begin_ref[...] = latest.astype(F32).T
        norm_ref[...] = jnp.zeros((TOK_DEV, DH), F32)

    query = lax.broadcasted_iota(I32, (TOK_DEV, TOK_DEV), 0)
    key = lax.broadcasted_iota(I32, (TOK_DEV, TOK_DEV), 1)
    allowed = (key <= query) & (key.astype(F32) >= begin_ref[:, :1])
    lane = lax.broadcasted_iota(I32, (TOK_DEV, DH), 1)
    queries, keys, values = (
        pick(selection, *(ref[...] for ref in part)) for part in (queries, keys, values)
    )
    for i in range(HB):
        columns = slice(i * DH, (i + 1) * DH)
        q_high, q_low = split(features(queries[:, columns], pair))
        k_high, k_low = split(features(keys[:, columns], pair))
        feature_ref[i, 0] = q_high
        feature_ref[i, 1] = q_low
        scores = dot_nt(q_high, k_high) + dot_nt(q_high, k_low) + dot_nt(q_low, k_high)
        s_high, s_low = split(jnp.where(allowed, scores, 0.0))
        value = jnp.concatenate(
            [values[:, columns].astype(BF16), jnp.ones((TOK_DEV, DH), BF16)], axis=1
        )
        total = dot(s_high, value) + dot(s_low, value)
        out_ref[i] = total[:, :DH]
        mine = lane == pl.program_id(0) * HB + i
        norm_ref[...] = jnp.where(mine, total[:, DH:], norm_ref[...])


def local_attention(where, lengths, nets, feature_map, rows, left, right, half, earlier=()):
    smem = pl.BlockSpec(memory_space=pltpu.SMEM)
    whole = lambda *shape: pl.BlockSpec(shape, lambda i: (0,) * len(shape))
    part = lambda *shape: pl.BlockSpec(shape, lambda i: (half,) + (0,) * (len(shape) - 1))
    specs = [spec for part_at in range(3) for spec in part_specs(part_at, half)]
    return pl.pallas_call(
        attention_kernel,
        out_shape=(
            pltpu.HBM((H, 2, TOK_DEV, M), BF16),
            pltpu.HBM((2, H // 2 + 1, TOK_DEV, DH), F32),
        ),
        grid=(1,),
        in_specs=[smem, smem, smem, whole(DH, M), *specs]
        + [pl.BlockSpec(memory_space=pl.ANY)] * len(earlier),
        out_specs=(part(H // 2, 2, TOK_DEV, M), part(1, H // 2 + 1, TOK_DEV, DH)),
        scratch_shapes=[pltpu.VMEM((TOK_DEV, 8), F32)] + selection_scratch(),
        input_output_aliases={13 + i: i for i in range(len(earlier))},
        compiler_params=pltpu.CompilerParams(vmem_limit_bytes=24 << 20),
        cost_estimate=pl.CostEstimate(
            flops=3_000_000_000, transcendentals=500_000, bytes_accessed=4_000_000
        ),
        name="local_attention",
    )(where, lengths, nets, in_hbm(feature_map), *([rows, left, right] * 3), *earlier)


def tail_kernel(where_ref, states_ref, out_ref):
    state, norm = decode(states_ref[0])
    for j in range(1, GROUP):
        keep = where_ref[4 + j] == 0
        more, more_norm = decode(states_ref[j])
        state = jnp.where(keep, state, 0.0) + more
        norm = jnp.where(keep, norm, 0.0) + more_norm
    out_ref[...] = encode(state, norm)


def group_tail(where, states):
    vmem = pl.BlockSpec(memory_space=pltpu.VMEM)
    return pl.pallas_call(
        tail_kernel,
        out_shape=jax.ShapeDtypeStruct((CODED, M), I16),
        in_specs=[pl.BlockSpec(memory_space=pltpu.SMEM), vmem],
        out_specs=vmem,
        name="group_tail",
    )(where, states)


def prefix_kernel(where_ref, states_ref, near_ref, far_ref, state_ref, norm_ref, out_ref, carried, sem):
    near, near_norm = decode(near_ref[...])
    far, far_norm = decode(far_ref[...])
    reaches = where_ref[2] == 0
    state = near + jnp.where(reaches, far, 0.0)
    norm = near_norm + jnp.where(reaches, far_norm, 0.0)
    head = where_ref[12]
    first = where_ref[3] != 0
    carried[...] = jnp.zeros_like(carried)

    @pl.when(first)
    def _():
        copy = pltpu.make_async_copy(state_ref.at[head], carried, sem)
        copy.start()
        copy.wait()

    mine = lax.broadcasted_iota(I32, (H, M), 0) == jnp.where(first, head, -1)
    norm = norm + jnp.sum(jnp.where(mine, norm_ref[...], 0.0), axis=0, keepdims=True)
    state = state + carried[...].T
    for j in range(GROUP):
        out_ref[j] = encode(state, norm)
        if j < GROUP - 1:
            keep = where_ref[4 + j] == 0
            more, more_norm = decode(states_ref[j])
            state = jnp.where(keep, state, 0.0) + more
            norm = jnp.where(keep, norm, 0.0) + more_norm


def entering_states(where, states, near, far, carried_state, carried_norm):
    vmem = pl.BlockSpec(memory_space=pltpu.VMEM)
    return pl.pallas_call(
        prefix_kernel,
        out_shape=jax.ShapeDtypeStruct((GROUP, CODED, M), I16),
        in_specs=[
            pl.BlockSpec(memory_space=pltpu.SMEM),
            vmem,
            vmem,
            vmem,
            pl.BlockSpec(memory_space=pl.ANY),
            vmem,
        ],
        out_specs=vmem,
        scratch_shapes=[pltpu.VMEM((M, DH), F32), pltpu.SemaphoreType.DMA(())],
        name="entering_states",
    )(where, states, in_hbm(near), in_hbm(far), in_hbm(carried_state), carried_norm)


def finish_kernel(where_ref, state_ref, feature_ref, local_ref, out_ref):
    carried = lax.broadcasted_iota(I32, (TOK_DEV, 1), 0) < where_ref[13]
    lane = lax.broadcasted_iota(I32, (TOK_DEV, DH), 1)
    norms = local_ref[0, H // 2]
    for i in range(H // 2):
        local_norm = jnp.sum(jnp.where(lane == i, norms, 0.0), axis=1, keepdims=True)
        state, norm = decode(state_ref[i])
        state = jnp.concatenate([state, jnp.broadcast_to(norm, (DH, M))], axis=0)
        s_high, s_low = split(state)
        q_high, q_low = feature_ref[i, 0], feature_ref[i, 1]
        entering = dot_nt(q_high, s_high) + dot_nt(q_high, s_low) + dot_nt(q_low, s_high)
        entering = jnp.where(carried, entering, 0.0)
        total = local_ref[0, i] + entering[:, :DH]
        out_ref[:, i * DH : (i + 1) * DH] = total / (local_norm + entering[:, DH:])


def finish(where, states, query_features, sums):
    half = H // 2
    part = lambda *shape: pl.BlockSpec(shape, lambda i: (i,) + (0,) * (len(shape) - 1))
    return pl.pallas_call(
        finish_kernel,
        out_shape=jax.ShapeDtypeStruct((TOK_DEV, H * DH), F32),
        grid=(2,),
        in_specs=[
            pl.BlockSpec(memory_space=pltpu.SMEM),
            part(half, CODED, M),
            part(half, 2, TOK_DEV, M),
            part(1, half + 1, TOK_DEV, DH),
        ],
        out_specs=pl.BlockSpec((TOK_DEV, half * DH), lambda i: (0, i)),
        compiler_params=pltpu.CompilerParams(vmem_limit_bytes=24 << 20),
        name="finish",
    )(where, states, in_hbm(query_features), in_hbm(sums))


def shifted(block, axis, count, distance):
    ahead = max(distance, 0)
    return lax.ppermute(
        block, axis, [(i - distance, i) for i in range(ahead, count + min(distance, 0))]
    )


def local(loader_rows, loader_lengths, net_lengths, feature_map, carried_state, carried_norm):
    device = lax.axis_index("grp") * SHARDS + lax.axis_index("seq")
    groups = [list(range(i, i + GROUP)) for i in range(0, SHARDS, GROUP)]

    tail, head, length = windows(loader_rows, loader_lengths)
    left = shifted(tail, "seq", SHARDS, 1)
    right = shifted(head, "seq", SHARDS, -1)
    lengths = lax.all_to_all(length, "seq", 0, 0, tiled=True)
    where = in_hbm(net_flags(device.astype(I32)[None], net_lengths))
    states = local_states(where, lengths, feature_map, loader_rows, left, right)
    states = lax.all_to_all(states, "seq", 0, 0, axis_index_groups=groups, tiled=True)
    attend = functools.partial(
        local_attention, where, lengths, net_lengths, feature_map, loader_rows, left, right
    )
    first = attend(0)
    states, *first = lax.optimization_barrier((states, *first))
    states = states.reshape(GROUP, CODED, M)
    tail = group_tail(where, states)
    far = shifted(tail, ("grp", "seq"), DEVICES, 2 * GROUP)
    near = shifted(tail, ("grp", "seq"), DEVICES, GROUP)
    states = entering_states(where, states, near, far, carried_state, carried_norm)
    states = lax.all_to_all(states, "seq", 0, 0, axis_index_groups=groups, tiled=True)
    return finish(where, states, *attend(1, first))


def solution(mesh):
    in_specs = (P(("grp", "seq"), None), P("grp", "seq"), P(), P(), P(), P())
    out_specs = P(("grp", "seq"), None)
    return jax.shard_map(local, mesh=mesh, in_specs=in_specs, out_specs=out_specs, check_vma=False)
```

```python
import functools

import jax
import jax.numpy as jnp
from jax import lax
from jax.experimental import pallas as pl
from jax.experimental.pallas import tpu as pltpu
from jax.sharding import PartitionSpec as P

H = 8
DH = 128
M = 256
TOK_DEV = 256
DRIFT = 96
CAP = 448
SHARDS = 32
DEVICES = 512
GROUP = 8
NETS = 64
TAIL = 104
REST = DRIFT + TAIL
LATER = 128
AUG = 136
CODED = 136
HB = 4
HALF = M // 2
F32 = jnp.float32
BF16 = jnp.bfloat16
I16 = jnp.int16
I32 = jnp.int32
TOP = 32768.0
NT = (((1,), (1,)), ((), ()))


def dot(a, b):
    return jnp.dot(a, b, preferred_element_type=F32)


def dot_nt(a, b):
    return lax.dot_general(a, b, NT, preferred_element_type=F32)


def in_hbm(x):
    return pltpu.with_memory_space_constraint(x, pltpu.HBM)


def split(x):
    high = x.astype(BF16)
    return high, (x - high.astype(F32)).astype(BF16)


def tail_start(length):
    start = jnp.maximum(length - DRIFT, 0)
    return jnp.minimum(start - lax.rem(start, 8), CAP - TAIL)


def windows_kernel(length_ref, rows_ref, tail_ref, head_ref, lengths_ref, sem):
    start = pl.multiple_of(tail_start(length_ref[0, 0]), 8)
    tail = pltpu.make_async_copy(rows_ref.at[pl.ds(start, TAIL), :], tail_ref, sem.at[0])
    head = pltpu.make_async_copy(rows_ref.at[pl.ds(0, DRIFT), :], head_ref, sem.at[1])
    tail.start()
    head.start()
    lengths_ref[...] = jnp.full((SHARDS, 1, 1), length_ref[0, 0], I32)
    tail.wait()
    head.wait()


def windows(rows, length):
    return pl.pallas_call(
        windows_kernel,
        out_shape=(
            jax.ShapeDtypeStruct((TAIL, 3 * H * DH), BF16),
            jax.ShapeDtypeStruct((DRIFT, 3 * H * DH), BF16),
            jax.ShapeDtypeStruct((SHARDS, 1, 1), I32),
        ),
        in_specs=[pl.BlockSpec(memory_space=pltpu.SMEM), pl.BlockSpec(memory_space=pl.ANY)],
        out_specs=[pl.BlockSpec(memory_space=pltpu.VMEM)] * 3,
        scratch_shapes=[pltpu.SemaphoreType.DMA((2,))],
        name="windows",
    )(length, rows)


def flags_kernel(place_ref, nets_ref, out_ref):
    device = place_ref[0]
    start = device * TOK_DEV
    member = lax.rem(device, GROUP)
    group_start = device - member
    for i in range(16):
        out_ref[i] = 0

    def one(n, carry):
        begin, last, first, nearby, earlier = carry
        begin = begin + nets_ref[n - 1]
        row = begin - start
        last = jnp.where(row < TOK_DEV, row, last)
        first = jnp.where(row >= 0, jnp.minimum(first, row), first)
        at = lax.shift_right_logical(begin, 8) - group_start
        inside = (at >= 0) & (at < GROUP)
        out_ref[jnp.where(inside, 4 + at, 15)] = 1
        nearby = jnp.where((at < 0) & (at >= -GROUP), 1, nearby)
        earlier = jnp.where(at < 0, 1, earlier)
        return begin, last, first, nearby, earlier

    zero = jnp.int32(0)
    _, last, first, nearby, earlier = lax.fori_loop(
        1, NETS, one, (zero, -1 - start, jnp.int32(TOK_DEV), zero, zero)
    )
    out_ref[0] = lax.rem(device, SHARDS)
    out_ref[1] = last
    out_ref[2] = nearby
    out_ref[3] = 1 - earlier
    out_ref[12] = member
    out_ref[13] = first
    out_ref[14] = start


def net_flags(place, net_lengths):
    smem = pl.BlockSpec(memory_space=pltpu.SMEM)
    return pl.pallas_call(
        flags_kernel,
        out_shape=jax.ShapeDtypeStruct((16,), I32),
        in_specs=[smem, smem],
        out_specs=smem,
        name="net_flags",
    )(place, net_lengths)


def exponent(top):
    return jnp.ceil(jnp.log2(jnp.maximum(top, 1e-30)))


def encode(state, norm):
    power = exponent(jnp.max(jnp.abs(state), axis=0, keepdims=True))
    codes = jnp.clip(jnp.round(state * jnp.exp2(15.0 - power)), 1.0 - TOP, TOP - 1.0)
    norm_power = exponent(norm)
    scaled = norm * jnp.exp2(15.0 - norm_power)
    high = jnp.minimum(jnp.round(scaled), TOP - 1.0)
    low = jnp.minimum(jnp.round((scaled - high) * TOP), TOP - 1.0)
    row = lax.broadcasted_iota(I32, (CODED - DH, state.shape[1]), 0)
    rest = jnp.where(row == 0, high, jnp.where(row == 1, low, jnp.where(row == 2, power, norm_power)))
    return jnp.concatenate([codes, rest], axis=0).astype(I32).astype(I16)


def decode(coded):
    codes = coded.astype(I32).astype(F32)
    high, low, power, norm_power = (codes[DH + i : DH + i + 1] for i in range(4))
    state = codes[:DH] * jnp.exp2(power - 15.0)
    return state, (high + low * (1.0 / TOP)) * jnp.exp2(norm_power - 15.0)


def build_selection(lengths_ref, seq_index, main_ref, rest_ref, drift_ref):
    before = lax.fori_loop(0, seq_index, lambda i, s: s + lengths_ref[i, 0, 0], jnp.int32(0))
    length = lengths_ref[seq_index, 0, 0]
    length_left = lengths_ref[jnp.maximum(seq_index - 1, 0), 0, 0]
    drift = before - seq_index * TOK_DEV
    drift_ref[0] = drift
    own = lax.broadcasted_iota(I32, (TOK_DEV, TOK_DEV), 0) - drift
    column = lax.broadcasted_iota(I32, (TOK_DEV, TOK_DEV), 1)
    main_ref[...] = jnp.where((column == own) & (own < length), 1.0, 0.0).astype(BF16)
    own = lax.broadcasted_iota(I32, (TOK_DEV, REST), 0) - drift
    column = lax.broadcasted_iota(I32, (TOK_DEV, REST), 1)
    late = jnp.where(drift >= 0, length_left - tail_start(length_left), -TOK_DEV)
    of_right = (own >= length) & (column == own - length) & (column < DRIFT)
    of_left = (column == own + late + DRIFT) & (column >= DRIFT)
    of_left = of_left & (own < jnp.where(drift >= 0, 0, length))
    rest_ref[...] = jnp.where(of_right | of_left, 1.0, 0.0).astype(BF16)


def pick(selection, own, left, right):
    main_ref, rest_ref, drift_ref = selection
    other = jnp.where(drift_ref[0] >= 0, left, own[TOK_DEV : TOK_DEV + TAIL])
    rest = jnp.concatenate([right, other], axis=0)
    return dot(main_ref[...], own[:TOK_DEV]) + dot(rest_ref[...], rest)


def feature_map_pair(map_ref, pair_ref):
    high, low = split(map_ref[...])
    pair_ref[:DH, :] = high
    pair_ref[DH:, :] = low


def features(part, pair_ref):
    scale = lax.rsqrt(jnp.mean(part * part, axis=-1, keepdims=True) + 1e-06) * DH ** (-0.5)
    twice = part.astype(BF16)
    return jnp.exp(dot(jnp.concatenate([twice, twice], axis=1), pair_ref[...]) * scale)


def state_kernel(
    where_ref, lengths_ref, map_ref, rows_ref, left_ref, right_ref, out_ref, pair, *selection
):
    build_selection(lengths_ref, where_ref[0], *selection)
    feature_map_pair(map_ref, pair)
    first = where_ref[1]
    valid = lax.broadcasted_iota(I32, (TOK_DEV, 1), 0) >= first
    norm_rows = jnp.where(
        lax.broadcasted_iota(I32, (AUG - DH, TOK_DEV), 1) >= first, 1.0, 0.0
    ).astype(BF16)
    width = HB * DH
    for at in range(H // HB):
        keys, values = (
            pick(
                selection,
                rows_ref[: TOK_DEV + LATER, start : start + width],
                left_ref[:, start : start + width],
                right_ref[:, start : start + width],
            )
            for start in (H * DH + at * width, 2 * H * DH + at * width)
        )
        for i in range(HB):
            columns = slice(i * DH, (i + 1) * DH)
            high, low = split(features(keys[:, columns], pair))
            masked = jnp.where(valid, values[:, columns], 0.0)
            turned = jnp.concatenate([masked.T.astype(BF16), norm_rows], axis=0)
            total = dot(turned, high) + dot(turned, low)
            out_ref[at * HB + i] = encode(total[:DH], total[DH : DH + 1])


def part_specs(part, first):
    column = part * (H // HB) + first
    return [
        pl.BlockSpec((TOK_DEV + LATER, HB * DH), lambda i, *_: (0, column + i)),
        pl.BlockSpec((TAIL, HB * DH), lambda i, *_: (0, column + i)),
        pl.BlockSpec((DRIFT, HB * DH), lambda i, *_: (0, column + i)),
    ]


def selection_scratch():
    return [
        pltpu.VMEM((2 * DH, M), BF16),
        pltpu.VMEM((TOK_DEV, TOK_DEV), BF16),
        pltpu.VMEM((TOK_DEV, REST), BF16),
        pltpu.SMEM((1,), I32),
    ]


def local_states(where, lengths, feature_map, rows, left, right):
    smem = pl.BlockSpec(memory_space=pltpu.SMEM)
    vmem = pl.BlockSpec(memory_space=pltpu.VMEM)
    whole = lambda *shape: pl.BlockSpec(shape, lambda i: (0,) * len(shape))
    return pl.pallas_call(
        state_kernel,
        out_shape=pltpu.HBM((H, CODED, M), I16),
        grid=(1,),
        in_specs=[smem, smem, whole(DH, M), vmem, vmem, whole(DRIFT, 3 * H * DH)],
        out_specs=whole(H, CODED, M),
        scratch_shapes=selection_scratch(),
        compiler_params=pltpu.CompilerParams(vmem_limit_bytes=24 << 20),
        name="local_states",
    )(where, lengths, in_hbm(feature_map), rows, left, right)


def attention_kernel(where_ref, lengths_ref, nets_ref, map_ref, *refs):
    queries, keys, values = refs[:3], refs[3:6], refs[6:9]
    feature_ref, sums_ref, begin_ref, pair, *selection = refs[-7:]
    out_ref = sums_ref.at[0]
    norm_ref = out_ref.at[H // 2]

    @pl.when(pl.program_id(0) == 0)
    def _():
        build_selection(lengths_ref, where_ref[0], *selection)
        feature_map_pair(map_ref, pair)
        row = lax.broadcasted_iota(I32, (8, TOK_DEV), 1)

        def one(n, carry):
            begin, latest = carry
            begin = begin + nets_ref[n - 1]
            return begin, jnp.where(row >= begin, begin, latest)

        start = where_ref[14]
        _, latest = lax.fori_loop(
            1, NETS, one, (-start, jnp.full((8, TOK_DEV), -1 - start, I32))
        )
        begin_ref[...] = latest.astype(F32).T
        norm_ref[...] = jnp.zeros((TOK_DEV, DH), F32)

    query = lax.broadcasted_iota(I32, (TOK_DEV, TOK_DEV), 0)
    key = lax.broadcasted_iota(I32, (TOK_DEV, TOK_DEV), 1)
    allowed = (key <= query) & (key.astype(F32) >= begin_ref[:, :1])
    lane = lax.broadcasted_iota(I32, (TOK_DEV, DH), 1)
    queries, keys, values = (
        pick(selection, *(ref[...] for ref in part)) for part in (queries, keys, values)
    )
    for i in range(HB):
        columns = slice(i * DH, (i + 1) * DH)
        q_high, q_low = split(features(queries[:, columns], pair))
        k_high, k_low = split(features(keys[:, columns], pair))
        feature_ref[i, 0] = q_high
        feature_ref[i, 1] = q_low
        scores = dot_nt(q_high, k_high) + dot_nt(q_high, k_low) + dot_nt(q_low, k_high)
        s_high, s_low = split(jnp.where(allowed, scores, 0.0))
        value = jnp.concatenate(
            [values[:, columns].astype(BF16), jnp.ones((TOK_DEV, DH), BF16)], axis=1
        )
        total = dot(s_high, value) + dot(s_low, value)
        out_ref[i] = total[:, :DH]
        mine = lane == pl.program_id(0) * HB + i
        norm_ref[...] = jnp.where(mine, total[:, DH:], norm_ref[...])


def local_attention(where, lengths, nets, feature_map, rows, left, right, half, earlier=()):
    smem = pl.BlockSpec(memory_space=pltpu.SMEM)
    whole = lambda *shape: pl.BlockSpec(shape, lambda i: (0,) * len(shape))
    part = lambda *shape: pl.BlockSpec(shape, lambda i: (half,) + (0,) * (len(shape) - 1))
    specs = [spec for part_at in range(3) for spec in part_specs(part_at, half)]
    return pl.pallas_call(
        attention_kernel,
        out_shape=(
            pltpu.HBM((H, 2, TOK_DEV, M), BF16),
            pltpu.HBM((2, H // 2 + 1, TOK_DEV, DH), F32),
        ),
        grid=(1,),
        in_specs=[smem, smem, smem, whole(DH, M), *specs]
        + [pl.BlockSpec(memory_space=pl.ANY)] * len(earlier),
        out_specs=(part(H // 2, 2, TOK_DEV, M), part(1, H // 2 + 1, TOK_DEV, DH)),
        scratch_shapes=[pltpu.VMEM((TOK_DEV, 8), F32)] + selection_scratch(),
        input_output_aliases={13 + i: i for i in range(len(earlier))},
        compiler_params=pltpu.CompilerParams(vmem_limit_bytes=24 << 20),
        cost_estimate=pl.CostEstimate(
            flops=3_000_000_000, transcendentals=500_000, bytes_accessed=4_000_000
        ),
        name="local_attention",
    )(where, lengths, nets, in_hbm(feature_map), *([rows, left, right] * 3), *earlier)


def tail_kernel(where_ref, states_ref, out_ref):
    state, norm = decode(states_ref[0])
    for j in range(1, GROUP):
        keep = where_ref[4 + j] == 0
        more, more_norm = decode(states_ref[j])
        state = jnp.where(keep, state, 0.0) + more
        norm = jnp.where(keep, norm, 0.0) + more_norm
    out_ref[...] = encode(state, norm)


def group_tail(where, states):
    vmem = pl.BlockSpec(memory_space=pltpu.VMEM)
    return pl.pallas_call(
        tail_kernel,
        out_shape=jax.ShapeDtypeStruct((CODED, M), I16),
        in_specs=[pl.BlockSpec(memory_space=pltpu.SMEM), vmem],
        out_specs=vmem,
        name="group_tail",
    )(where, states)


def prefix_kernel(where_ref, states_ref, near_ref, far_ref, state_ref, norm_ref, out_ref, carried, sem):
    near, near_norm = decode(near_ref[...])
    far, far_norm = decode(far_ref[...])
    reaches = where_ref[2] == 0
    state = near + jnp.where(reaches, far, 0.0)
    norm = near_norm + jnp.where(reaches, far_norm, 0.0)
    head = where_ref[12]
    first = where_ref[3] != 0
    carried[...] = jnp.zeros_like(carried)

    @pl.when(first)
    def _():
        copy = pltpu.make_async_copy(state_ref.at[head], carried, sem)
        copy.start()
        copy.wait()

    mine = lax.broadcasted_iota(I32, (H, M), 0) == jnp.where(first, head, -1)
    norm = norm + jnp.sum(jnp.where(mine, norm_ref[...], 0.0), axis=0, keepdims=True)
    state = state + carried[...].T
    for j in range(GROUP):
        out_ref[j] = encode(state, norm)
        if j < GROUP - 1:
            keep = where_ref[4 + j] == 0
            more, more_norm = decode(states_ref[j])
            state = jnp.where(keep, state, 0.0) + more
            norm = jnp.where(keep, norm, 0.0) + more_norm


def entering_states(where, states, near, far, carried_state, carried_norm):
    vmem = pl.BlockSpec(memory_space=pltpu.VMEM)
    return pl.pallas_call(
        prefix_kernel,
        out_shape=pltpu.HBM((GROUP, CODED, M), I16),
        grid=(1,),
        in_specs=[
            pl.BlockSpec(memory_space=pltpu.SMEM),
            vmem,
            vmem,
            vmem,
            pl.BlockSpec(memory_space=pl.ANY),
            vmem,
        ],
        out_specs=pl.BlockSpec((GROUP, CODED, M), lambda i: (0, 0, 0)),
        scratch_shapes=[pltpu.VMEM((M, DH), F32), pltpu.SemaphoreType.DMA(())],
        compiler_params=pltpu.CompilerParams(vmem_limit_bytes=24 << 20),
        name="entering_states",
    )(where, states, near, far, in_hbm(carried_state), carried_norm)


def finish_kernel(where_ref, state_ref, feature_ref, local_ref, out_ref):
    carried = lax.broadcasted_iota(I32, (TOK_DEV, 1), 0) < where_ref[13]
    lane = lax.broadcasted_iota(I32, (TOK_DEV, DH), 1)
    norms = local_ref[0, H // 2]
    for i in range(H // 2):
        local_norm = jnp.sum(jnp.where(lane == i, norms, 0.0), axis=1, keepdims=True)
        state, norm = decode(state_ref[i])
        state = jnp.concatenate([state, jnp.broadcast_to(norm, (DH, M))], axis=0)
        s_high, s_low = split(state)
        q_high, q_low = feature_ref[i, 0], feature_ref[i, 1]
        entering = dot_nt(q_high, s_high) + dot_nt(q_high, s_low) + dot_nt(q_low, s_high)
        entering = jnp.where(carried, entering, 0.0)
        total = local_ref[0, i] + entering[:, :DH]
        out_ref[:, i * DH : (i + 1) * DH] = total / (local_norm + entering[:, DH:])


def finish(where, states, query_features, sums):
    half = H // 2
    part = lambda *shape: pl.BlockSpec(shape, lambda i: (i,) + (0,) * (len(shape) - 1))
    return pl.pallas_call(
        finish_kernel,
        out_shape=jax.ShapeDtypeStruct((TOK_DEV, H * DH), F32),
        grid=(2,),
        in_specs=[
            pl.BlockSpec(memory_space=pltpu.SMEM),
            part(half, CODED, M),
            part(half, 2, TOK_DEV, M),
            part(1, half + 1, TOK_DEV, DH),
        ],
        out_specs=pl.BlockSpec((TOK_DEV, half * DH), lambda i: (0, i)),
        compiler_params=pltpu.CompilerParams(vmem_limit_bytes=24 << 20),
        name="finish",
    )(where, states, in_hbm(query_features), in_hbm(sums))


def shifted(block, axis, count, distance):
    ahead = max(distance, 0)
    return lax.ppermute(
        block, axis, [(i - distance, i) for i in range(ahead, count + min(distance, 0))]
    )


def local(loader_rows, loader_lengths, net_lengths, feature_map, carried_state, carried_norm):
    device = lax.axis_index("grp") * SHARDS + lax.axis_index("seq")
    groups = [list(range(i, i + GROUP)) for i in range(0, SHARDS, GROUP)]

    tail, head, length = windows(loader_rows, loader_lengths)
    left = shifted(tail, "seq", SHARDS, 1)
    right = shifted(head, "seq", SHARDS, -1)
    lengths = lax.all_to_all(length, "seq", 0, 0, tiled=True)
    where = in_hbm(net_flags(device.astype(I32)[None], net_lengths))
    states = local_states(where, lengths, feature_map, loader_rows, left, right)
    states = lax.all_to_all(states, "seq", 0, 0, axis_index_groups=groups, tiled=True)
    attend = functools.partial(
        local_attention, where, lengths, net_lengths, feature_map, loader_rows, left, right
    )
    first = attend(0)
    states, *first = lax.optimization_barrier((states, *first))
    states = states.reshape(GROUP, CODED, M)
    tail = group_tail(where, states)
    far = shifted(tail, ("grp", "seq"), DEVICES, 2 * GROUP)
    near = shifted(tail, ("grp", "seq"), DEVICES, GROUP)
    states = entering_states(where, states, near, far, carried_state, carried_norm)
    states = lax.all_to_all(states, "seq", 0, 0, axis_index_groups=groups, tiled=True)
    return finish(where, states, *attend(1, first))


def solution(mesh):
    in_specs = (P(("grp", "seq"), None), P("grp", "seq"), P(), P(), P(), P())
    out_specs = P(("grp", "seq"), None)
    return jax.shard_map(local, mesh=mesh, in_specs=in_specs, out_specs=out_specs, check_vma=False)
```
